512 devices in a mesh: group: 32 (over x, y_lo, core), pos: 16 (over z, y_hi).
Axes of the slice: x: 4, y: 8 (y_hi: 2, y_lo: 4; y = y_hi * 4 + y_lo), z: 8, core: 2. Of those that a mesh axis runs over, the one named last changes fastest.
Arguments:
- potential: float32 [4, 2, 6144, 2048], P(None, None, 'group', 'pos'), may hold values from -0.3 to 0.3
- probe: float32 [32, 4, 128, 256], P('group', None, 'pos'), may hold values from -3 to 3
- amplitudes: bfloat16 [32, 16, 3, 128, 128], P('group', 'pos'), may hold values from 0.1 to 8, as said below
- row_offset: int32 [32, 16, 3], P('group', 'pos'), may hold values from 0 to 64
- col_offset: int32 [32, 16, 3], P('group', 'pos'), may hold values from 0 to 127
- counts: int32 [32, 16], P('group', 'pos'), may hold values from 1 to 3, as said below
Outputs:
- object_grad: float32 [4, 2, 6144, 2048], P(None, None, 'group', 'pos')
- probe_grad: float32 [32, 4, 128, 256], P('group', None, 'pos')
The draws below stay inside these ranges and needn't reach their ends.
Inputs may be any that keep to these rules, and one draw needn't show every extreme that they name: A tile's positions fill its first counts slots and later slots are unused; at least one tile has 3. `amplitudes`: every entry is positive.
All inputs are finite; a program needn't handle non-finite values.
Results may differ from the reference program's by a relative error of at most 0.02.
The reference program's roundings to bfloat16 on the way count: a program that leaves them out, or rounds other values in their place, can miss the bound.
Values sent between devices are 32-bit elements; how exact they have to be, the bound alone decides.
A program may use at most 64 MiB of HBM per device.

```python
import math
import jax
import jax.numpy as jnp
from jax import lax

N = 128
MODES = 4
SLICES = 4
PMAX = 3
ROWS = 192
GROUPS = 32
TILES = 16


def draw_counts(key, part):
    base = jax.random.randint(jax.random.fold_in(key, 11), (GROUPS, TILES), 1, PMAX + 1)
    spot = jax.random.randint(jax.random.fold_in(key, 12), (2,), 0, 1 << 20)
    return base.at[spot[0] % GROUPS, spot[1] % TILES].set(PMAX).astype(jnp.int32)


def draw_amplitudes(key, part):
    place = jnp.arange(GROUPS * TILES, dtype=jnp.float32).reshape(GROUPS, TILES)
    fraction = place / max(GROUPS * TILES - 1, 1)
    tile_odd = (jnp.arange(TILES, dtype=jnp.int32) % 2).astype(jnp.float32)[None, :]
    slot_first = (jnp.arange(PMAX, dtype=jnp.int32) == 0).astype(jnp.float32)
    baseline = jax.random.uniform(jax.random.fold_in(key, 22), (GROUPS, TILES, PMAX, N, N), jnp.float32, 0.25, 1.25)
    factor = (1.0 + 2.0 * fraction) * (1.0 + tile_odd)
    slot_factor = 2.0 - slot_first
    value = baseline * factor[:, :, None, None, None] * slot_factor[None, None, :, None, None]
    return jnp.clip(value, 0.1, 8.0).astype(jnp.bfloat16)


def touch_ends(entries, rng, smallest, top_value):
    extent = entries.shape
    index_at = [jax.random.randint(jax.random.fold_in(rng, axis), (), 0, extent[axis]) for axis in range(len(extent))]
    entries = entries.at[tuple(index_at)].set(smallest)
    longest = extent.index(max(extent))
    index_at[longest] = (index_at[longest] + 1) % extent[longest]
    return entries.at[tuple(index_at)].set(top_value)


def steps_of(key, extent, split, least, top_value):
    loudness, own = 1.0, jax.random.fold_in(key, 6)
    for position, blocks in split:
        draws = jnp.exp(jax.random.uniform(jax.random.fold_in(own, position), (blocks,), jnp.float32, least / len(split), top_value / len(split)))
        loudness = loudness * jnp.repeat(draws, extent[position] // blocks).reshape([-1 if axis == position else 1 for axis in range(len(extent))])
    return loudness


def noise(key, dims, spread, bound, cuts=(), kind=jnp.bfloat16):
    level = steps_of(key, dims, cuts, -0.22, 0.18) if cuts else 1.0
    values = jax.random.normal(key, dims, jnp.float32) * spread * level
    return jnp.minimum(jnp.maximum(values, -bound), bound).astype(kind)


def setup_inputs(seed: int = 0) -> dict:
    key_of = jax.random.split(jax.random.key(seed), 7)
    potential = jnp.clip(jax.random.uniform(key_of[0], (SLICES, 2, GROUPS * ROWS, TILES * N), jnp.float32, -0.3, 0.3) * steps_of(key_of[0], (SLICES, 2, GROUPS * ROWS, TILES * N), ((2, 32), (3, 16)), -0.4, 0.0), -0.3, 0.3)
    probe = noise(key_of[1], (GROUPS, MODES, N, 2 * N), 0.5, 3.0, ((0, 32), (2, 16)), jnp.float32)
    amplitudes = draw_amplitudes(jax.random.fold_in(key_of[6], 71), 0)
    row_offset = touch_ends(jax.random.randint(key_of[3], (GROUPS, TILES, PMAX), 0, ROWS - N + 1), jax.random.fold_in(key_of[3], 1), 0, ROWS - N).astype(jnp.int32)
    col_offset = touch_ends(jax.random.randint(key_of[4], (GROUPS, TILES, PMAX), 0, N), jax.random.fold_in(key_of[4], 1), 0, N - 1).astype(jnp.int32)
    counts = draw_counts(jax.random.fold_in(key_of[6], 71), 0)
    return dict(potential=potential, probe=probe, amplitudes=amplitudes, row_offset=row_offset, col_offset=col_offset, counts=counts)


PROP = 0.25
REG = 0.1

def tables(size):
    idx = jnp.arange(size, dtype=jnp.int32)
    prod = idx[:, None] * idx[None, :] % size
    angle = 2.0 * math.pi / size * prod.astype(jnp.float32)
    cosv = jnp.cos(angle) / math.sqrt(size)
    sinv = jnp.sin(angle) / math.sqrt(size)
    forward = jnp.concatenate([jnp.concatenate([cosv, -sinv], 1), jnp.concatenate([sinv, cosv], 1)], 0)
    inverse = jnp.concatenate([jnp.concatenate([cosv, sinv], 1), jnp.concatenate([-sinv, cosv], 1)], 0)
    return (forward.astype(jnp.bfloat16), inverse.astype(jnp.bfloat16))

def propagator(size):
    idx = jnp.arange(size, dtype=jnp.int32)
    freq = jnp.where(idx < size // 2, idx, idx - size).astype(jnp.float32)
    phase = -2.0 * math.pi * PROP / size * (freq[:, None] * freq[:, None] + freq[None, :] * freq[None, :])
    return jnp.concatenate([jnp.cos(phase), jnp.sin(phase)], 1)

def along_last(wave, table):
    size = wave.shape[-2]
    flat = wave.reshape(-1, 2 * size).astype(jnp.bfloat16).astype(jnp.float32)
    out = jnp.dot(flat, table.astype(jnp.float32), precision=lax.Precision.HIGHEST, preferred_element_type=jnp.float32)
    return out.reshape(wave.shape)

def flip(wave):
    lead = wave.shape[:-2]
    size = wave.shape[-2]
    parts = wave.reshape(lead + (size, 2, size))
    return jnp.swapaxes(parts, -3, -1).reshape(lead + (size, 2 * size))

def transform(wave, table):
    return flip(along_last(flip(along_last(wave, table)), table))

def cmul(left, right):
    size = left.shape[-2]
    lre, lim = (left[..., :size], left[..., size:])
    rre, rim = (right[..., :size], right[..., size:])
    return jnp.concatenate([lre * rre - lim * rim, lre * rim + lim * rre], -1)

def cmulc(left, right):
    size = left.shape[-2]
    lre, lim = (left[..., :size], left[..., size:])
    rre, rim = (right[..., :size], right[..., size:])
    return jnp.concatenate([lre * rre + lim * rim, lre * rim - lim * rre], -1)

def transmit(patch):
    magnitude = jnp.exp(-patch[:, 1])
    return jnp.concatenate([magnitude * jnp.cos(patch[:, 0]), magnitude * jnp.sin(patch[:, 0])], -1)

def potential_grad(trans, tgrad):
    size = trans.shape[-2]
    quot = cmulc(trans, tgrad)
    return jnp.stack([quot[:, size:], -quot[:, :size]], 0)

def one_position(carry, extended, whole, observed, row, col, weight, forward, inverse, kernel):
    grad_ext, probe_acc, misfit = carry
    slices = extended.shape[0]
    size = whole.shape[-2]
    zero = jnp.zeros((), jnp.int32)
    start = (zero, zero, row.astype(jnp.int32), col.astype(jnp.int32))
    patch = lax.dynamic_slice(extended, start, (slices, 2, size, size))
    trans = transmit(patch)
    psi = whole
    stored = []
    exit_wave = psi
    for layer in range(slices):
        stored.append(psi)
        exit_wave = cmul(trans[layer][None], psi)
        if layer + 1 < slices:
            psi = transform(cmul(kernel[None], transform(exit_wave, forward)), inverse)
    far = transform(exit_wave, forward)
    real_part, imag_part = (far[..., :size], far[..., size:])
    inten = lax.optimization_barrier(jnp.sum(real_part * real_part + imag_part * imag_part, axis=0))
    model = jnp.sqrt(inten + REG)
    diff = model - observed
    misfit = misfit + weight * jnp.sum(diff * diff)
    ratio = weight * (1.0 - observed / model)
    wave_grad = transform(far * jnp.concatenate([ratio, ratio], -1)[None], inverse)
    pieces = [None] * slices
    psi_grad = wave_grad
    for layer in reversed(range(slices)):
        tgrad = lax.optimization_barrier(jnp.sum(cmulc(stored[layer], wave_grad), axis=0))
        pieces[layer] = potential_grad(trans[layer], tgrad)
        psi_grad = cmulc(trans[layer][None], wave_grad)
        if layer > 0:
            wave_grad = transform(cmulc(kernel[None], transform(psi_grad, forward)), inverse)
    block = jnp.stack(pieces, 0)
    old = lax.dynamic_slice(grad_ext, start, block.shape)
    grad_ext = lax.dynamic_update_slice(grad_ext, old + block, start)
    return (grad_ext, probe_acc + psi_grad, misfit)

def reference(potential, probe, amplitudes, row_offset, col_offset, counts):
    slices = potential.shape[0]
    size = probe.shape[2]
    groups, tiles = counts.shape
    slots = amplitudes.shape[2]
    rows_tile = potential.shape[2] // groups
    padded = jnp.pad(potential, ((0, 0), (0, 0), (0, 0), (0, size)))
    forward, inverse = tables(size)
    kernel = propagator(size)
    zero = jnp.zeros((), jnp.int32)

    def device(index, carry):
        grad_pad, probe_grads, misfit = carry
        index = index.astype(jnp.int32)
        grp = index // tiles
        til = index % tiles
        start = (zero, zero, (grp * rows_tile).astype(jnp.int32), (til * size).astype(jnp.int32))
        extended = lax.dynamic_slice(padded, start, (slices, 2, rows_tile, 2 * size))
        whole = lax.dynamic_index_in_dim(probe, grp, 0, keepdims=False)
        amps = amplitudes[grp, til].astype(jnp.float32)
        rows_here = row_offset[grp, til]
        cols_here = col_offset[grp, til]
        count = counts[grp, til]

        def slot_step(slot, inner):
            weight = (slot < count).astype(jnp.float32)
            return one_position(inner, extended, whole, amps[slot], rows_here[slot], cols_here[slot], weight, forward, inverse, kernel)
        init = (jnp.zeros((slices, 2, rows_tile, 2 * size), jnp.float32), jnp.zeros(whole.shape, jnp.float32), jnp.zeros((), jnp.float32))
        grad_ext, probe_acc, local = lax.fori_loop(0, slots, slot_step, init)
        old = lax.dynamic_slice(grad_pad, start, grad_ext.shape)
        grad_pad = lax.dynamic_update_slice(grad_pad, old + grad_ext, start)
        old_probe = lax.dynamic_index_in_dim(probe_grads, grp, 0, keepdims=False)
        probe_grads = lax.dynamic_update_index_in_dim(probe_grads, old_probe + probe_acc, grp, 0)
        return (grad_pad, probe_grads, misfit + local)
    init = (jnp.zeros(padded.shape, jnp.float32), jnp.zeros(probe.shape, jnp.float32), jnp.zeros((), jnp.float32))
    grad_pad, probe_grads, misfit = lax.fori_loop(0, groups * tiles, device, init)
    total = jnp.sum(counts).astype(jnp.float32)
    scale = 1.0 / jnp.sqrt(misfit / (total * size * size) + 1e-06)
    return (grad_pad[..., :tiles * size] * scale, probe_grads * scale)
```

```python
import math

import jax
import jax.numpy as jnp
import numpy as np
from jax import lax
from jax.experimental import pallas as pl
from jax.experimental.pallas import tpu as pltpu
from jax.sharding import PartitionSpec as P

PROP = 0.25
REG = 0.1
N = 128
MODES = 4
SLICES = 4
SLOTS = 3
ROWS = 192
XS, YL, ZS = 4, 4, 8
F32 = jnp.float32
BF16 = jnp.bfloat16


def tables():
    idx = np.arange(N, dtype=np.int32)
    prod = (idx[:, None] * idx[None, :] % N).astype(np.float32)
    angle = np.float32(2.0 * math.pi / N) * prod
    root = np.float32(math.sqrt(N))
    cosv = np.cos(angle.astype(np.float64)).astype(np.float32) / root
    sinv = np.sin(angle.astype(np.float64)).astype(np.float32) / root
    forward = np.concatenate([np.concatenate([cosv, -sinv], 1), np.concatenate([sinv, cosv], 1)], 0)
    inverse = np.concatenate([np.concatenate([cosv, sinv], 1), np.concatenate([-sinv, cosv], 1)], 0)
    return jnp.asarray(forward).astype(BF16), jnp.asarray(inverse).astype(BF16)


def propagator():
    idx = np.arange(N, dtype=np.int32)
    freq = np.where(idx < N // 2, idx, idx - N).astype(np.float32)
    factor = np.float32(-2.0 * math.pi * PROP / N)
    phase = factor * (freq[:, None] * freq[:, None] + freq[None, :] * freq[None, :])
    phase = phase.astype(np.float32).astype(np.float64)
    return jnp.asarray(np.concatenate([np.cos(phase), np.sin(phase)], 1).astype(np.float32))


def cmul(a, b):
    return a[0] * b[0] - a[1] * b[1], a[0] * b[1] + a[1] * b[0]


def cmulc(a, b):
    return a[0] * b[0] + a[1] * b[1], a[0] * b[1] - a[1] * b[0]


def dft(waves, right, left):
    rows = [jnp.concatenate([re.astype(BF16), im.astype(BF16)], 1) for re, im in waves]
    first = jnp.dot(jnp.concatenate(rows, 0), right, preferred_element_type=F32).astype(BF16)
    cols = []
    for m in range(len(waves)):
        part = first[m * N : (m + 1) * N]
        cols.append(jnp.concatenate([part[:, :N], part[:, N:]], 0))
    second = jnp.dot(left, jnp.concatenate(cols, 1), preferred_element_type=F32)
    return [(second[:N, m * N : (m + 1) * N], second[N:, m * N : (m + 1) * N]) for m in range(len(waves))]


def kernel(
    pot, probe, amps_in, row_in, col_in, cnt_in, fwd_in, inv_in, kern_in,
    out_obj, out_probe,
    n0, n1, n2, n3, c0, c1, c2, c3, gn, gc, rbuf, xbuf, sbuf, amps, amps_out, metav, meta_out, meta,
    pbuf, psi0, psi, wav, tr, gp, pacc, pgr, px, pzr, pown, pfin,
    mis, misr, smis,
    loc_sem, s_misc, r_probe, r_meta, r_amp,
    s_n, r_n, s_c, r_c, s_f, r_f, s_pz, r_pz, s_pf, r_pf,
    s_x, r_x, s_r, r_r, s_rn, r_rn, s_px, r_px, s_pq, r_pq, s_po, r_po, s_m, r_m,
):
    nbuf = (n0, n1, n2, n3)
    cbuf = (c0, c1, c2, c3)
    g = lax.axis_index("group")
    pos = lax.axis_index("pos")
    x, yl, c = g // 8, (g // 2) % 4, g % 2
    z, h = pos // 2, pos % 2
    oh = 1 - h
    oc = 1 - c
    nat = c == h
    guest = c != h
    keep = jnp.where(nat, 0, 1)
    give = 1 - keep
    dz = jnp.where(h == 0, ZS - 1, 1)

    def dev(xx, yy, hh, zz, cc):
        return {"group": xx * 8 + yy * 2 + cc, "pos": zz * 2 + hh}

    def remote(src, dst, send, recv, to):
        return pltpu.make_async_remote_copy(src_ref=src, dst_ref=dst, send_sem=send, recv_sem=recv, device_id=to)

    def at_z(k):
        return lax.rem(z + k, ZS)

    sibling = dev(x, yl, h, z, oc)
    ring_z = [dev(x, yl, h, at_z(k), c) for k in range(1, ZS)]
    ring_y = []
    for k in range(1, 8):
        y = lax.rem(h * 4 + yl + k, 8)
        ring_y.append(dev(x, y % 4, y // 4, z, c))
    ring_x = []
    for k in range(1, 8):
        q = lax.rem(x * 2 + c + k, 8)
        ring_x.append(dev(q // 2, yl, h, z, q % 2))
    partners = ring_z + ring_y + ring_x
    partners += [dev(x, yl, oh, z, oc), dev(x, yl, h, at_z(1), oc), dev(x, yl, h, at_z(ZS - 1), oc)]

    barrier = pltpu.get_barrier_semaphore()
    for partner in partners:
        pl.semaphore_signal(barrier, inc=1, device_id=partner)

    lane = lax.broadcasted_iota(jnp.int32, (8, N), 1)
    packed = jnp.zeros((8, N), jnp.int32)
    for p in range(SLOTS):
        packed = jnp.where(lane == p, row_in[0, 0, p], packed)
        packed = jnp.where(lane == SLOTS + p, col_in[0, 0, p], packed)
    packed = jnp.where(lane == 2 * SLOTS, cnt_in[0, 0], packed)
    meta_out[...] = packed
    for p in range(SLOTS):
        amps_out[p] = amps_in[0, 0, p].astype(F32)
    gp[...] = jnp.zeros_like(gp)

    pl.semaphore_wait(barrier, len(partners))

    to_probe = remote(probe.at[0], pbuf.at[h, z], s_misc.at[0], r_probe, dev(x, yl, oh, z, oc))
    to_meta = remote(meta_out, metav, s_misc.at[1], r_meta, dev(x, yl, oh, z, 1))
    to_amp = remote(amps_out, amps, s_misc.at[2], r_amp, dev(x, yl, oh, z, 1))
    to_metan = remote(meta_out, metav, s_misc.at[1], r_meta, dev(x, yl, h, at_z(1), 0))
    to_ampn = remote(amps_out, amps, s_misc.at[2], r_amp, dev(x, yl, h, at_z(1), 0))
    to_n = [remote(pot.at[s], nbuf[s], s_n.at[s], r_n.at[s], dev(x, yl, h, lax.rem(z + dz, ZS), oc)) for s in range(SLICES)]
    to_c = [
        [remote(pot.at[s, ch], cbuf[s].at[ch], s_c.at[s, ch], r_c.at[s], dev(x, yl, oh, z, c if ch == 0 else oc)) for ch in range(2)]
        for s in range(SLICES)
    ]
    own_probe = [remote(probe.at[0], pbuf.at[c, z], s_pz.at[k], r_pz.at[k], ring_z[k]) for k in range(ZS - 1)]
    got_probe = [remote(pbuf.at[c, z], pbuf.at[c, z], s_pz.at[k], r_pz.at[k], ring_z[k]) for k in range(ZS - 1)]
    loc_n = [pltpu.make_async_copy(pot.at[s], nbuf[s], loc_sem.at[s]) for s in range(SLICES)]
    loc_p = pltpu.make_async_copy(probe.at[0], pbuf.at[c, z], loc_sem.at[4])
    loc_a = pltpu.make_async_copy(amps_out, amps, loc_sem.at[5])
    loc_m = pltpu.make_async_copy(meta_out, metav, loc_sem.at[6])
    loc_s = pltpu.make_async_copy(metav, meta, loc_sem.at[7])
    here = jnp.logical_and(nat, h == 0)
    along = jnp.logical_and(nat, h == 1)

    @pl.when(guest)
    def _():
        to_probe.start()
        to_meta.start()
        for s in range(SLICES):
            for ch in range(2):
                to_c[s][ch].start()
        to_amp.start()

    @pl.when(nat)
    def _():
        for k in (0, 6, 1, 5, 2, 4, 3):
            own_probe[k].start()
        loc_p.start()
        for s in range(SLICES):
            loc_n[s].start()

    @pl.when(along)
    def _():
        to_metan.start()

    @pl.when(here)
    def _():
        loc_a.start()
        loc_m.start()

    @pl.when(nat)
    def _():
        for s in range(SLICES):
            to_n[s].start()

    @pl.when(along)
    def _():
        to_ampn.start()

    @pl.when(here)
    def _():
        loc_m.wait()

    @pl.when(jnp.logical_not(here))
    def _():
        to_meta.wait_recv()

    loc_s.start()

    @pl.when(guest)
    def _():
        to_probe.wait_recv()
        for k in (0, 6, 1, 5, 2, 4, 3):
            got_probe[k].start()

    @pl.when(nat)
    def _():
        loc_p.wait()

    loc_s.wait()

    fwd_c = [remote(cbuf[s].at[keep], cbuf[s].at[keep], s_f.at[s], r_f.at[s], sibling) for s in range(SLICES)]
    got_c = [remote(cbuf[s].at[keep], cbuf[s].at[keep], s_f.at[s], r_c.at[s], sibling) for s in range(SLICES)]

    def pass_on(s):
        got_c[s].wait_recv()
        fwd_c[s].start()

    last = jnp.logical_or(
        jnp.logical_and(jnp.logical_and(h == 0, c == 1), z == ZS - 1),
        jnp.logical_and(jnp.logical_and(h == 1, c == 0), z == 0),
    )
    alive = jnp.where(last, 0, 1)

    def masks(p, rows):
        col = meta[0, SLOTS + p]
        spot = lax.broadcasted_iota(jnp.int32, (rows, N), 1)
        n_lo = jnp.where(c == 0, col, 0)
        n_hi = jnp.where(c == 0, N, col * alive)
        c_lo = jnp.where(c == 0, 0, col)
        c_hi = jnp.where(c == 0, col * alive, N)
        in_n = jnp.logical_and(spot >= n_lo, spot < n_hi)
        in_c = jnp.logical_and(spot >= c_lo, spot < c_hi)
        return in_n, in_c, col

    def transmit(s):
        @pl.when(nat)
        def _():
            loc_n[s].wait()

        @pl.when(guest)
        def _():
            to_n[s].wait_recv()

        fwd_c[s].wait_recv()

        def one(p, carry):
            in_n, in_c, col = masks(p, N)
            row = meta[0, p]
            shift = lax.rem(N - col, N)
            parts = []
            for ch in range(2):
                near = nbuf[s][ch, pl.ds(row, N), :]
                far = cbuf[s][ch, pl.ds(row, N), :]
                both = jnp.where(in_n, near, jnp.where(in_c, far, 0.0))
                parts.append(pltpu.roll(both, shift, 1))
            mag = jnp.exp(-parts[1])
            tr[s, p, 0] = mag * jnp.cos(parts[0])
            tr[s, p, 1] = mag * jnp.sin(parts[0])
            return carry

        lax.fori_loop(0, SLOTS, one, 0)

    def pair(ref, *at):
        return ref[(*at, slice(None), slice(0, N))], ref[(*at, slice(None), slice(N, 2 * N))]

    def put(ref, value, *at):
        ref[(*at, slice(None), slice(0, N))] = value[0]
        ref[(*at, slice(None), slice(N, 2 * N))] = value[1]

    def psi_at(s, p, m):
        return pair(psi0, m) if s == 0 else pair(psi, s - 1, p, m)

    def trans_at(s, p):
        return tr[s, p, 0], tr[s, p, 1]

    def prop(s):
        def one(p, carry):
            t = trans_at(s, p)
            kern = pair(kern_in)
            waves = dft([cmul(t, psi_at(s, p, m)) for m in range(MODES)], fwd_in[...], inv_in[...])
            waves = dft([cmul(kern, w) for w in waves], inv_in[...], fwd_in[...])
            for m in range(MODES):
                put(psi, waves[m], s, p, m)
            return carry

        lax.fori_loop(0, SLOTS, one, 0)

    pass_on(0)
    transmit(0)
    for k in range(ZS - 1):
        own_probe[k].wait_recv()
    fwd_p = remote(pbuf.at[c], pbuf.at[c], s_pf, r_pf, sibling)
    fwd_p.start()
    pass_on(1)
    fwd_p.wait_recv()
    for zz in range(ZS):
        for hh in range(2):
            at = (2 * zz + hh) * 8
            for m in range(MODES):
                psi0[m, at : at + 8, :] = pbuf[hh, zz, m]
    prop(0)
    pass_on(2)
    transmit(1)
    prop(1)
    pass_on(3)
    transmit(2)
    prop(2)
    transmit(3)

    @pl.when(here)
    def _():
        loc_a.wait()

    @pl.when(jnp.logical_not(here))
    def _():
        to_amp.wait_recv()

    count = meta[0, 2 * SLOTS]
    mis[0:8, :] = jnp.zeros((8, N), F32)
    mis[8:16, :] = jnp.zeros((8, N), F32) + count.astype(F32)

    def detect(p, carry):
        weight = jnp.where(p < count, 1.0, 0.0)
        t = trans_at(SLICES - 1, p)
        far = dft([cmul(t, psi_at(SLICES - 1, p, m)) for m in range(MODES)], fwd_in[...], inv_in[...])
        inten = far[0][0] * far[0][0] + far[0][1] * far[0][1]
        for m in range(1, MODES):
            inten = inten + (far[m][0] * far[m][0] + far[m][1] * far[m][1])
        model = jnp.sqrt(inten + REG)
        seen = amps[p]
        diff = model - seen
        sq = weight * (diff * diff)
        part = sq[0:8]
        for r in range(1, N // 8):
            part = part + sq[r * 8 : r * 8 + 8]
        mis[0:8, :] = mis[0:8, :] + part
        ratio = weight * (1.0 - seen / model)
        waves = dft([(w[0] * ratio, w[1] * ratio) for w in far], inv_in[...], fwd_in[...])
        for m in range(MODES):
            put(wav, waves[m], p, m)
        return carry

    lax.fori_loop(0, SLOTS, detect, 0)

    def spread(step, ring):
        return [remote(smis.at[step], misr.at[step, k], s_m.at[step, k], r_m.at[step, k], ring[k]) for k in range(7)]

    spreads = [spread(i, ring) for i, ring in enumerate((ring_z, ring_y, ring_x))]

    def send_mis(step):
        smis[step] = mis[...]
        for q in spreads[step]:
            q.start()

    def take_mis(step):
        total = mis[...]
        for k, q in enumerate(spreads[step]):
            q.wait_recv()
            total = total + misr[step, k]
        mis[...] = total

    send_mis(0)

    give_x = [remote(gc.at[s, give], xbuf.at[s], s_x.at[s], r_x.at[s], sibling) for s in range(SLICES)]
    send_r = [remote(sbuf.at[s], rbuf.at[s, keep], s_r.at[s], r_r.at[s, keep], dev(x, yl, oh, z, h)) for s in range(SLICES)]
    got_r = [[remote(sbuf.at[s], rbuf.at[s, ch], s_r.at[s], r_r.at[s, ch], sibling) for ch in range(2)] for s in range(SLICES)]
    send_rn = [remote(gn.at[s], rbuf.at[s], s_rn.at[s], r_rn.at[s], dev(x, yl, h, lax.rem(z + ZS - dz, ZS), h)) for s in range(SLICES)]

    def patch_grad(s):
        gn[s] = jnp.zeros((2, ROWS, N), F32)
        gc[s] = jnp.zeros((2, ROWS, N), F32)

        def one(p, carry):
            t = trans_at(s, p)
            parts = [cmulc(psi_at(s, p, m), pair(wav, p, m)) for m in range(MODES)]
            tg = (parts[0][0] + parts[1][0] + parts[2][0] + parts[3][0], parts[0][1] + parts[1][1] + parts[2][1] + parts[3][1])
            q = cmulc(t, tg)
            in_n, in_c, col = masks(p, ROWS)
            row = meta[0, p]
            for ch, value in enumerate((q[1], -q[0])):
                gp[ch, 64 : 64 + N, :] = pltpu.roll(value, col, 1)
                placed = gp[ch, pl.ds(64 - row, ROWS), :]
                gn[s, ch] = gn[s, ch] + jnp.where(in_n, placed, 0.0)
                gc[s, ch] = gc[s, ch] + jnp.where(in_c, placed, 0.0)
            return carry

        lax.fori_loop(0, SLOTS, one, 0)
        give_x[s].start()

        @pl.when(guest)
        def _():
            send_rn[s].start()

    def back(s):
        def one(p, carry):
            t = trans_at(s, p)
            kern = pair(kern_in)
            waves = dft([cmulc(t, pair(wav, p, m)) for m in range(MODES)], fwd_in[...], inv_in[...])
            waves = dft([cmulc(kern, w) for w in waves], inv_in[...], fwd_in[...])
            for m in range(MODES):
                put(wav, waves[m], p, m)
            return carry

        lax.fori_loop(0, SLOTS, one, 0)

    def hand_over(s):
        give_x[s].wait_recv()
        sbuf[s] = gc[s, keep] + xbuf[s]
        send_r[s].start()

    for s in reversed(range(1, SLICES)):
        patch_grad(s)
        back(s)
        hand_over(s)
        if s == 3:
            take_mis(0)
            send_mis(1)
        if s == 2:
            take_mis(1)
            send_mis(2)
    patch_grad(0)

    pacc[...] = jnp.zeros_like(pacc)

    def probe_slot(p, carry):
        t = trans_at(0, p)
        for m in range(MODES):
            w = cmulc(t, pair(wav, p, m))
            put(pacc, (pacc[m, :, 0:N] + w[0], pacc[m, :, N : 2 * N] + w[1]), m)
        return carry

    lax.fori_loop(0, SLOTS, probe_slot, 0)
    for zz in range(ZS):
        for hh in range(2):
            at = (2 * zz + hh) * 8
            for m in range(MODES):
                pgr[hh, zz, m] = pacc[m, at : at + 8, :]
    give_p = remote(pgr.at[oc], px, s_px, r_px, sibling)
    give_p.start()
    hand_over(0)
    give_p.wait_recv()
    px[...] = px[...] + pgr[c]
    send_q = [remote(px.at[at_z(k)], pzr.at[k - 1], s_pq.at[k - 1], r_pq.at[k - 1], ring_z[k - 1]) for k in range(1, ZS)]
    for k in (3, 2, 4, 1, 5, 0, 6):
        send_q[k].start()
    take_mis(2)
    total = mis[...]
    misfit = jnp.sum(jnp.sum(total[0:8], axis=0, keepdims=True), axis=1, keepdims=True)
    slots = total[8:9, 0:1]
    scale = 1.0 / jnp.sqrt(misfit / (slots * N * N) + 1e-06)
    for q in send_q:
        q.wait_recv()
    done = px[z]
    for k in range(ZS - 1):
        done = done + pzr[k]
    pfin[...] = done
    send_po = remote(pfin, pown, s_po, r_po, dev(x, yl, oh, z, h))

    @pl.when(guest)
    def _():
        send_po.start()

    @pl.when(nat)
    def _():
        out_probe[0] = pfin[...] * scale
        for s in reversed(range(SLICES)):
            send_rn[s].wait_recv()
            out_obj[s] = (gn[s] + rbuf[s]) * scale

    @pl.when(guest)
    def _():
        for s in reversed(range(SLICES)):
            for ch in range(2):
                got_r[s][ch].wait_recv()
            out_obj[s] = rbuf[s] * scale
        send_po.wait_recv()
        out_probe[0] = pown[...] * scale

    @pl.when(guest)
    def _():
        to_probe.wait_send()
        to_meta.wait_send()
        to_amp.wait_send()
        for s in range(SLICES):
            for ch in range(2):
                to_c[s][ch].wait_send()
            send_rn[s].wait_send()
        send_po.wait_send()

    @pl.when(nat)
    def _():
        for s in range(SLICES):
            to_n[s].wait_send()

    @pl.when(along)
    def _():
        to_metan.wait_send()
        to_ampn.wait_send()

    for k in range(ZS - 1):
        own_probe[k].wait_send()
        send_q[k].wait_send()
        for step in range(3):
            spreads[step][k].wait_send()
    fwd_p.wait_send()
    give_p.wait_send()
    for s in range(SLICES):
        fwd_c[s].wait_send()
        give_x[s].wait_send()
        send_r[s].wait_send()


def body(potential, probe, amplitudes, row_offset, col_offset, counts):
    forward, inverse = tables()
    kern = propagator()
    vmem = pl.BlockSpec(memory_space=pltpu.VMEM)
    smem = pl.BlockSpec(memory_space=pltpu.SMEM)
    hbm = pl.BlockSpec(memory_space=pl.ANY)
    dma = pltpu.SemaphoreType.DMA
    tile = (SLICES, 2, ROWS, N)
    wave = (MODES, N, 2 * N)
    chunk = (MODES, 8, 2 * N)

    def f32(*shape):
        return pltpu.VMEM(shape, F32)

    return pl.pallas_call(
        kernel,
        out_shape=(jax.ShapeDtypeStruct(tile, F32), jax.ShapeDtypeStruct((1, *chunk), F32)),
        in_specs=[hbm, hbm, vmem, smem, smem, smem, vmem, vmem, vmem],
        out_specs=(vmem, vmem),
        scratch_shapes=[
            *[f32(*tile[1:])] * 8, f32(*tile), f32(*tile), f32(*tile),
            f32(SLICES, ROWS, N), f32(SLICES, ROWS, N),
            f32(SLOTS, N, N), f32(SLOTS, N, N),
            pltpu.VMEM((8, N), jnp.int32), pltpu.VMEM((8, N), jnp.int32), pltpu.SMEM((8, N), jnp.int32),
            f32(2, ZS, *chunk), f32(*wave), f32(SLICES - 1, SLOTS, *wave), f32(SLOTS, *wave),
            f32(SLICES, SLOTS, 2, N, N), f32(2, 256, N),
            f32(*wave), f32(2, ZS, *chunk), f32(ZS, *chunk), f32(ZS - 1, *chunk), f32(*chunk), f32(*chunk),
            f32(16, N), f32(3, 7, 16, N), f32(3, 16, N),
            dma((8,)), dma((3,)), dma, dma, dma,
            dma((4,)), dma((4,)), dma((4, 2)), dma((4,)), dma((4,)), dma((4,)),
            dma((7,)), dma((7,)), dma, dma,
            dma((4,)), dma((4,)), dma((4,)), dma((4, 2)), dma((4,)), dma((4,)),
            dma, dma, dma((7,)), dma((7,)), dma, dma, dma((3, 7)), dma((3, 7)),
        ],
        compiler_params=pltpu.CompilerParams(collective_id=0, has_side_effects=True),
        name="ptycho",
    )(potential, probe, amplitudes, row_offset, col_offset, counts, forward, inverse, kern)


def solution(mesh):
    placed = (
        P(None, None, "group", "pos"),
        P("group", None, "pos", None),
        P("group", "pos", None, None, None),
        P("group", "pos", None),
        P("group", "pos", None),
        P("group", "pos"),
    )
    return jax.shard_map(
        body,
        mesh=mesh,
        in_specs=placed,
        out_specs=(P(None, None, "group", "pos"), P("group", None, "pos", None)),
        check_vma=False,
    )
```

```python
import math

import jax
import jax.numpy as jnp
import numpy as np
from jax import lax
from jax.experimental import pallas as pl
from jax.experimental.pallas import tpu as pltpu
from jax.sharding import PartitionSpec as P

PROP = 0.25
REG = 0.1
N = 128
MODES = 4
SLICES = 4
SLOTS = 3
ROWS = 192
XS, YL, ZS = 4, 4, 8
F32 = jnp.float32
BF16 = jnp.bfloat16


def tables():
    idx = np.arange(N, dtype=np.int32)
    prod = (idx[:, None] * idx[None, :] % N).astype(np.float32)
    angle = np.float32(2.0 * math.pi / N) * prod
    root = np.float32(math.sqrt(N))
    cosv = np.cos(angle.astype(np.float64)).astype(np.float32) / root
    sinv = np.sin(angle.astype(np.float64)).astype(np.float32) / root
    forward = np.concatenate([np.concatenate([cosv, -sinv], 1), np.concatenate([sinv, cosv], 1)], 0)
    inverse = np.concatenate([np.concatenate([cosv, sinv], 1), np.concatenate([-sinv, cosv], 1)], 0)
    return jnp.asarray(forward).astype(BF16), jnp.asarray(inverse).astype(BF16)


def propagator():
    idx = np.arange(N, dtype=np.int32)
    freq = np.where(idx < N // 2, idx, idx - N).astype(np.float32)
    factor = np.float32(-2.0 * math.pi * PROP / N)
    phase = factor * (freq[:, None] * freq[:, None] + freq[None, :] * freq[None, :])
    phase = phase.astype(np.float32).astype(np.float64)
    return jnp.asarray(np.concatenate([np.cos(phase), np.sin(phase)], 1).astype(np.float32))


def cmul(a, b):
    return a[0] * b[0] - a[1] * b[1], a[0] * b[1] + a[1] * b[0]


def cmulc(a, b):
    return a[0] * b[0] + a[1] * b[1], a[0] * b[1] - a[1] * b[0]


def dft(waves, right, left):
    rows = [jnp.concatenate([re.astype(BF16), im.astype(BF16)], 1) for re, im in waves]
    first = jnp.dot(jnp.concatenate(rows, 0), right, preferred_element_type=F32).astype(BF16)
    cols = []
    for m in range(len(waves)):
        part = first[m * N : (m + 1) * N]
        cols.append(jnp.concatenate([part[:, :N], part[:, N:]], 0))
    second = jnp.dot(left, jnp.concatenate(cols, 1), preferred_element_type=F32)
    return [(second[:N, m * N : (m + 1) * N], second[N:, m * N : (m + 1) * N]) for m in range(len(waves))]


def kernel(
    pot, probe, amps_in, row_in, col_in, cnt_in, fwd_hbm, inv_hbm, kern_hbm,
    out_obj, out_probe, out_scale,
    n0, n1, n2, n3, c0, c1, c2, c3, gn, gc, rbuf, xbuf, sbuf, amps, amps_out, metav, meta_out, meta,
    pbuf, psi, wav, tr, gp, pgr, px, pzr, pown, pfin,
    mis, misr, smis, stage, chunk, stage_sem, amps_raw, fwd_in, inv_in, kern_in,
    loc_sem, s_misc, r_probe, r_meta, r_amp,
    s_n, r_n, s_c, r_c, s_f, r_f, s_pz, r_pz, s_pf, r_pf,
    s_x, r_x, s_r, r_r, s_rn, r_rn, s_px, r_px, s_pq, r_pq, s_po, r_po, s_m, r_m,
):
    nbuf = (n0, n1, n2, n3)
    cbuf = (c0, c1, c2, c3)
    g = lax.axis_index("group")
    pos = lax.axis_index("pos")
    x, yl, c = g // 8, (g // 2) % 4, g % 2
    z, h = pos // 2, pos % 2
    oh = 1 - h
    oc = 1 - c
    nat = c == h
    guest = c != h
    keep = jnp.where(nat, 0, 1)
    give = 1 - keep
    dz = jnp.where(h == 0, ZS - 1, 1)

    def dev(xx, yy, hh, zz, cc):
        return {"group": xx * 8 + yy * 2 + cc, "pos": zz * 2 + hh}

    def remote(src, dst, send, recv, to):
        return pltpu.make_async_remote_copy(src_ref=src, dst_ref=dst, send_sem=send, recv_sem=recv, device_id=to)

    def at_z(k):
        return lax.rem(z + k, ZS)

    sibling = dev(x, yl, h, z, oc)
    ring_z = [dev(x, yl, h, at_z(k), c) for k in range(1, ZS)]
    ring_y = []
    for k in range(1, 8):
        y = lax.rem(h * 4 + yl + k, 8)
        ring_y.append(dev(x, y % 4, y // 4, z, c))
    ring_x = []
    for k in range(1, 8):
        q = lax.rem(x * 2 + c + k, 8)
        ring_x.append(dev(q // 2, yl, h, z, q % 2))
    partners = ring_z + ring_y + ring_x
    partners += [dev(x, yl, oh, z, oc), dev(x, yl, h, at_z(1), oc), dev(x, yl, h, at_z(ZS - 1), oc)]

    barrier = pltpu.get_barrier_semaphore()
    for partner in partners:
        pl.semaphore_signal(barrier, inc=1, device_id=partner)

    own_pot = [pltpu.make_async_copy(pot.at[s], stage.at[s], stage_sem.at[s]) for s in range(SLICES)]
    own_p = pltpu.make_async_copy(probe.at[0], chunk, stage_sem.at[4])
    own_p.start()
    for s in range(SLICES):
        own_pot[s].start()

    lane = lax.broadcasted_iota(jnp.int32, (8, N), 1)
    packed = jnp.zeros((8, N), jnp.int32)
    for p in range(SLOTS):
        packed = jnp.where(lane == p, row_in[0, 0, p], packed)
        packed = jnp.where(lane == SLOTS + p, col_in[0, 0, p], packed)
    packed = jnp.where(lane == 2 * SLOTS, cnt_in[0, 0], packed)
    meta_out[...] = packed
    own_a = pltpu.make_async_copy(amps_in.at[0, 0], amps_raw, stage_sem.at[5])
    consts = [pltpu.make_async_copy(src, dst, stage_sem.at[6 + i]) for i, (src, dst) in enumerate(((fwd_hbm, fwd_in), (inv_hbm, inv_in), (kern_hbm, kern_in)))]
    own_a.start()
    for q in consts:
        q.start()

    pl.semaphore_wait(barrier, len(partners))

    def half_of(ref, hh):
        return ref.at[:, :, pl.ds(pl.multiple_of(hh * 8, 8), 8), :]

    def chunk_of(ref, zz, hh):
        return ref.at[:, zz, pl.ds(pl.multiple_of(hh * 8, 8), 8), :]

    to_probe = remote(chunk, chunk_of(pbuf, z, h), s_misc.at[0], r_probe, dev(x, yl, oh, z, oc))
    to_meta = remote(meta_out, metav, s_misc.at[1], r_meta, dev(x, yl, oh, z, 1))
    to_amp = remote(amps_out, amps, s_misc.at[2], r_amp, dev(x, yl, oh, z, 1))
    to_metan = remote(meta_out, metav, s_misc.at[1], r_meta, dev(x, yl, h, at_z(1), 0))
    to_ampn = remote(amps_out, amps, s_misc.at[2], r_amp, dev(x, yl, h, at_z(1), 0))
    to_n = [remote(stage.at[s], nbuf[s], s_n.at[s], r_n.at[s], dev(x, yl, h, lax.rem(z + dz, ZS), oc)) for s in range(SLICES)]
    to_c = [
        [remote(stage.at[s, ch], cbuf[s].at[ch], s_c.at[s, ch], r_c.at[s], dev(x, yl, oh, z, c if ch == 0 else oc)) for ch in range(2)]
        for s in range(SLICES)
    ]
    own_probe = [remote(chunk, chunk_of(pbuf, z, c), s_pz.at[k], r_pz.at[k], ring_z[k]) for k in range(ZS - 1)]
    got_probe = [remote(chunk_of(pbuf, z, c), chunk_of(pbuf, z, c), s_pz.at[k], r_pz.at[k], ring_z[k]) for k in range(ZS - 1)]
    loc_n = [pltpu.make_async_copy(stage.at[s], nbuf[s], loc_sem.at[s]) for s in range(SLICES)]
    loc_p = pltpu.make_async_copy(chunk, chunk_of(pbuf, z, c), loc_sem.at[4])
    loc_a = pltpu.make_async_copy(amps_out, amps, loc_sem.at[5])
    loc_m = pltpu.make_async_copy(meta_out, metav, loc_sem.at[6])
    loc_s = pltpu.make_async_copy(metav, meta, loc_sem.at[7])
    here = jnp.logical_and(nat, h == 0)
    along = jnp.logical_and(nat, h == 1)

    @pl.when(guest)
    def _():
        to_meta.start()

    @pl.when(along)
    def _():
        to_metan.start()

    @pl.when(here)
    def _():
        loc_m.start()

    own_p.wait()

    @pl.when(guest)
    def _():
        to_probe.start()

    own_pot[0].wait()

    @pl.when(guest)
    def _():
        for ch in range(2):
            to_c[0][ch].start()

    @pl.when(nat)
    def _():
        to_n[0].start()
        for k in (0, 6, 1, 5, 2, 4, 3):
            own_probe[k].start()
        loc_p.start()
        loc_n[0].start()

    for s in range(1, SLICES):
        own_pot[s].wait()

        @pl.when(guest)
        def _(s=s):
            for ch in range(2):
                to_c[s][ch].start()

        @pl.when(nat)
        def _(s=s):
            loc_n[s].start()

    own_a.wait()
    for p in range(SLOTS):
        amps_out[p] = amps_raw[p].astype(F32)

    @pl.when(guest)
    def _():
        to_amp.start()

    @pl.when(here)
    def _():
        loc_a.start()

    gp[...] = jnp.zeros_like(gp)
    for q in consts:
        q.wait()

    @pl.when(here)
    def _():
        loc_m.wait()

    @pl.when(jnp.logical_not(here))
    def _():
        to_meta.wait_recv()

    loc_s.start()

    @pl.when(guest)
    def _():
        to_probe.wait_recv()
        for k in (0, 6, 1, 5, 2, 4, 3):
            got_probe[k].start()

    @pl.when(nat)
    def _():
        loc_p.wait()

    loc_s.wait()

    fwd_c = [remote(cbuf[s].at[keep], cbuf[s].at[keep], s_f.at[s], r_f.at[s], sibling) for s in range(SLICES)]
    got_c = [remote(cbuf[s].at[keep], cbuf[s].at[keep], s_f.at[s], r_c.at[s], sibling) for s in range(SLICES)]

    def pass_on(s):
        got_c[s].wait_recv()
        fwd_c[s].start()

    last = jnp.logical_or(
        jnp.logical_and(jnp.logical_and(h == 0, c == 1), z == ZS - 1),
        jnp.logical_and(jnp.logical_and(h == 1, c == 0), z == 0),
    )
    alive = jnp.where(last, 0, 1)

    def masks(p, rows):
        col = meta[0, SLOTS + p]
        spot = lax.broadcasted_iota(jnp.int32, (rows, N), 1)
        n_lo = jnp.where(c == 0, col, 0)
        n_hi = jnp.where(c == 0, N, col * alive)
        c_lo = jnp.where(c == 0, 0, col)
        c_hi = jnp.where(c == 0, col * alive, N)
        in_n = jnp.logical_and(spot >= n_lo, spot < n_hi)
        in_c = jnp.logical_and(spot >= c_lo, spot < c_hi)
        return in_n, in_c, col

    def transmit(s):
        @pl.when(nat)
        def _():
            loc_n[s].wait()

        @pl.when(guest)
        def _():
            to_n[s].wait_recv()

        fwd_c[s].wait_recv()

        def one(p, carry):
            in_n, in_c, col = masks(p, N)
            row = meta[0, p]
            shift = lax.rem(N - col, N)
            parts = []
            for ch in range(2):
                near = nbuf[s][ch, pl.ds(row, N), :]
                far = cbuf[s][ch, pl.ds(row, N), :]
                both = jnp.where(in_n, near, jnp.where(in_c, far, 0.0))
                parts.append(pltpu.roll(both, shift, 1))
            mag = jnp.exp(-parts[1])
            tr[s, p, 0] = mag * jnp.cos(parts[0])
            tr[s, p, 1] = mag * jnp.sin(parts[0])
            return carry

        lax.fori_loop(0, SLOTS, one, 0)

    def pair(ref, *at):
        return ref[(*at, slice(None), slice(0, N))], ref[(*at, slice(None), slice(N, 2 * N))]

    def put(ref, value, *at):
        ref[(*at, slice(None), slice(0, N))] = value[0]
        ref[(*at, slice(None), slice(N, 2 * N))] = value[1]

    def psi_at(s, p, m):
        if s:
            return pair(psi, s - 1, p, m)
        whole = pbuf[m].reshape(N, 2 * N)
        return whole[:, 0:N], whole[:, N : 2 * N]

    def trans_at(s, p):
        return tr[s, p, 0], tr[s, p, 1]

    def prop(s):
        def one(p, carry):
            t = trans_at(s, p)
            kern = pair(kern_in)
            waves = dft([cmul(t, psi_at(s, p, m)) for m in range(MODES)], fwd_in[...], inv_in[...])
            waves = dft([cmul(kern, w) for w in waves], inv_in[...], fwd_in[...])
            for m in range(MODES):
                put(psi, waves[m], s, p, m)
            return carry

        lax.fori_loop(0, SLOTS, one, 0)

    pass_on(0)

    @pl.when(nat)
    def _():
        to_n[1].start()

    transmit(0)
    for k in range(ZS - 1):
        own_probe[k].wait_recv()
    fwd_p = remote(half_of(pbuf, c), half_of(pbuf, c), s_pf, r_pf, sibling)
    fwd_p.start()
    pass_on(1)
    fwd_p.wait_recv()

    @pl.when(nat)
    def _():
        for s in range(2, SLICES):
            to_n[s].start()

    @pl.when(along)
    def _():
        to_ampn.start()

    prop(0)
    pass_on(2)
    transmit(1)
    prop(1)
    pass_on(3)
    transmit(2)
    prop(2)
    transmit(3)

    count = meta[0, 2 * SLOTS]
    mis[0:8, :] = jnp.zeros((8, N), F32)
    mis[8:16, :] = jnp.zeros((8, N), F32) + count.astype(F32)

    def spectrum(p, carry):
        t = trans_at(SLICES - 1, p)
        far = dft([cmul(t, psi_at(SLICES - 1, p, m)) for m in range(MODES)], fwd_in[...], inv_in[...])
        for m in range(MODES):
            put(wav, far[m], p, m)
        return carry

    lax.fori_loop(0, SLOTS, spectrum, 0)

    @pl.when(here)
    def _():
        loc_a.wait()

    @pl.when(jnp.logical_not(here))
    def _():
        to_amp.wait_recv()

    def detect(p, carry):
        weight = jnp.where(p < count, 1.0, 0.0)
        far = [pair(wav, p, m) for m in range(MODES)]
        inten = far[0][0] * far[0][0] + far[0][1] * far[0][1]
        for m in range(1, MODES):
            inten = inten + (far[m][0] * far[m][0] + far[m][1] * far[m][1])
        model = jnp.sqrt(inten + REG)
        seen = amps[p]
        diff = model - seen
        sq = weight * (diff * diff)
        part = sq[0:8]
        for r in range(1, N // 8):
            part = part + sq[r * 8 : r * 8 + 8]
        mis[0:8, :] = mis[0:8, :] + part
        ratio = weight * (1.0 - seen / model)
        waves = dft([(w[0] * ratio, w[1] * ratio) for w in far], inv_in[...], fwd_in[...])
        for m in range(MODES):
            put(wav, waves[m], p, m)
        return carry

    lax.fori_loop(0, SLOTS, detect, 0)

    def spread(step, ring):
        return [remote(smis.at[step], misr.at[step, k], s_m.at[step, k], r_m.at[step, k], ring[k]) for k in range(7)]

    spreads = [spread(i, ring) for i, ring in enumerate((ring_z, ring_x, ring_y))]

    def send_mis(step):
        smis[step] = mis[...]
        for q in spreads[step]:
            q.start()

    def take_mis(step):
        total = mis[...]
        for k, q in enumerate(spreads[step]):
            q.wait_recv()
            total = total + misr[step, k]
        mis[...] = total

    send_mis(0)

    give_x = [remote(gc.at[s, give], xbuf.at[s], s_x.at[s], r_x.at[s], sibling) for s in range(SLICES)]
    send_r = [remote(sbuf.at[s], rbuf.at[s, keep], s_r.at[s], r_r.at[s, keep], dev(x, yl, oh, z, h)) for s in range(SLICES)]
    got_r = [[remote(sbuf.at[s], rbuf.at[s, ch], s_r.at[s], r_r.at[s, ch], sibling) for ch in range(2)] for s in range(SLICES)]
    send_rn = [remote(gn.at[s], rbuf.at[s], s_rn.at[s], r_rn.at[s], dev(x, yl, h, lax.rem(z + ZS - dz, ZS), h)) for s in range(SLICES)]

    def patch_grad(s):
        gn[s] = jnp.zeros((2, ROWS, N), F32)
        gc[s] = jnp.zeros((2, ROWS, N), F32)

        def one(p, carry):
            t = trans_at(s, p)
            parts = [cmulc(psi_at(s, p, m), pair(wav, p, m)) for m in range(MODES)]
            tg = (parts[0][0] + parts[1][0] + parts[2][0] + parts[3][0], parts[0][1] + parts[1][1] + parts[2][1] + parts[3][1])
            q = cmulc(t, tg)
            in_n, in_c, col = masks(p, ROWS)
            row = meta[0, p]
            for ch, value in enumerate((q[1], -q[0])):
                gp[ch, 64 : 64 + N, :] = pltpu.roll(value, col, 1)
                placed = gp[ch, pl.ds(64 - row, ROWS), :]
                gn[s, ch] = gn[s, ch] + jnp.where(in_n, placed, 0.0)
                gc[s, ch] = gc[s, ch] + jnp.where(in_c, placed, 0.0)
            return carry

        lax.fori_loop(0, SLOTS, one, 0)
        give_x[s].start()

        @pl.when(jnp.logical_and(guest, s > 0))
        def _():
            send_rn[s].start()

    def back(s):
        def one(p, carry):
            t = trans_at(s, p)
            kern = pair(kern_in)
            waves = dft([cmulc(t, pair(wav, p, m)) for m in range(MODES)], fwd_in[...], inv_in[...])
            waves = dft([cmulc(kern, w) for w in waves], inv_in[...], fwd_in[...])
            for m in range(MODES):
                put(wav, waves[m], p, m)
            return carry

        lax.fori_loop(0, SLOTS, one, 0)

    def hand_over(s):
        give_x[s].wait_recv()
        sbuf[s] = gc[s, keep] + xbuf[s]
        send_r[s].start()

    for s in reversed(range(1, SLICES)):
        patch_grad(s)
        back(s)
        hand_over(s)
        if s == 2:
            take_mis(0)
            send_mis(1)

    pgr[...] = jnp.zeros_like(pgr)

    def probe_slot(p, carry):
        t = trans_at(0, p)
        for m in range(MODES):
            w = jnp.concatenate(cmulc(t, pair(wav, p, m)), 1)
            pgr[m] = pgr[m] + w.reshape(ZS, 16, 2 * N)
        return carry

    lax.fori_loop(0, SLOTS, probe_slot, 0)
    give_p = remote(half_of(pgr, oc), px, s_px, r_px, sibling)
    give_p.start()
    patch_grad(0)
    give_p.wait_recv()
    px[...] = px[...] + pgr[:, :, pl.ds(pl.multiple_of(c * 8, 8), 8), :]
    send_q = [remote(px.at[:, at_z(k)], pzr.at[k - 1], s_pq.at[k - 1], r_pq.at[k - 1], ring_z[k - 1]) for k in range(1, ZS)]
    for k in (3, 2, 4, 1, 5, 0, 6):
        send_q[k].start()

    @pl.when(guest)
    def _():
        send_rn[0].start()

    hand_over(0)
    take_mis(1)
    send_mis(2)
    for q in send_q:
        q.wait_recv()
    done = px[:, z]
    for k in range(ZS - 1):
        done = done + pzr[k]
    send_po = remote(pfin, pown, s_po, r_po, dev(x, yl, oh, z, h))

    @pl.when(guest)
    def _():
        pfin[...] = done
        send_po.start()

    out_n = [pltpu.make_async_copy(gn.at[s], out_obj.at[s], loc_sem.at[s]) for s in range(SLICES)]
    out_r = [pltpu.make_async_copy(rbuf.at[s], out_obj.at[s], loc_sem.at[s]) for s in range(SLICES)]

    @pl.when(nat)
    def _():
        out_probe[0] = done
        for s in reversed(range(SLICES)):
            send_rn[s].wait_recv()
            gn[s] = gn[s] + rbuf[s]
            out_n[s].start()

    @pl.when(guest)
    def _():
        for s in reversed(range(SLICES)):
            for ch in range(2):
                got_r[s][ch].wait_recv()
            out_r[s].start()
        send_po.wait_recv()
        out_probe[0] = pown[...]

    take_mis(2)
    total = mis[...]
    misfit = jnp.sum(jnp.sum(total[0:8], axis=0, keepdims=True), axis=1, keepdims=True)
    slots = total[8:9, 0:1]
    out_scale[...] = jnp.broadcast_to(1.0 / jnp.sqrt(misfit / (slots * N * N) + 1e-06), (8, N))

    @pl.when(guest)
    def _():
        to_probe.wait_send()
        to_meta.wait_send()
        to_amp.wait_send()
        for s in range(SLICES):
            for ch in range(2):
                to_c[s][ch].wait_send()
            send_rn[s].wait_send()
        send_po.wait_send()

    @pl.when(nat)
    def _():
        for s in range(SLICES):
            to_n[s].wait_send()

    @pl.when(along)
    def _():
        to_metan.wait_send()
        to_ampn.wait_send()

    for k in range(ZS - 1):
        own_probe[k].wait_send()
        send_q[k].wait_send()
        for step in range(3):
            spreads[step][k].wait_send()
    fwd_p.wait_send()
    give_p.wait_send()
    for s in range(SLICES):
        out_n[s].wait()
        fwd_c[s].wait_send()
        give_x[s].wait_send()
        send_r[s].wait_send()


def finish(obj, pgrad, scale, out_obj, out_probe, held, held_probe, factor, in_sem, out_sem):
    loads = [pltpu.make_async_copy(scale, factor, in_sem.at[SLICES])]
    loads += [pltpu.make_async_copy(obj.at[s], held.at[s], in_sem.at[s]) for s in range(SLICES)]
    loads.append(pltpu.make_async_copy(pgrad, held_probe, in_sem.at[SLICES + 1]))
    stores = [pltpu.make_async_copy(held.at[s], out_obj.at[s], out_sem.at[s]) for s in range(SLICES)]
    stores.append(pltpu.make_async_copy(held_probe, out_probe, out_sem.at[SLICES]))
    for load in loads:
        load.start()
    loads[0].wait()
    by = factor[0:1, 0:1]
    for s in range(SLICES):
        loads[s + 1].wait()
        held[s] = held[s] * by
        stores[s].start()
    loads[-1].wait()
    held_probe[...] = held_probe[...] * by
    stores[-1].start()
    for store in stores:
        store.wait()


def body(potential, probe, amplitudes, row_offset, col_offset, counts):
    forward, inverse = tables()
    kern = propagator()
    vmem = pl.BlockSpec(memory_space=pltpu.VMEM)
    smem = pl.BlockSpec(memory_space=pltpu.SMEM)
    hbm = pl.BlockSpec(memory_space=pltpu.HBM)
    dma = pltpu.SemaphoreType.DMA
    tile = (SLICES, 2, ROWS, N)
    wave = (MODES, N, 2 * N)
    chunk = (MODES, 8, 2 * N)

    def f32(*shape):
        return pltpu.VMEM(shape, F32)

    obj, pgrad, scale = pl.pallas_call(
        kernel,
        out_shape=tuple(jax.ShapeDtypeStruct(shape, F32) for shape in (tile, (1, *chunk), (8, N))),
        in_specs=[hbm, hbm, hbm, smem, smem, smem, hbm, hbm, hbm],
        out_specs=(hbm, vmem, vmem),
        scratch_shapes=[
            *[f32(*tile[1:])] * 8, f32(*tile), f32(*tile), f32(*tile),
            f32(SLICES, ROWS, N), f32(SLICES, ROWS, N),
            f32(SLOTS, N, N), f32(SLOTS, N, N),
            pltpu.VMEM((8, N), jnp.int32), pltpu.VMEM((8, N), jnp.int32), pltpu.SMEM((8, N), jnp.int32),
            f32(MODES, ZS, 16, 2 * N), f32(SLICES - 1, SLOTS, *wave), f32(SLOTS, *wave),
            f32(SLICES, SLOTS, 2, N, N), f32(2, 256, N),
            f32(MODES, ZS, 16, 2 * N), f32(MODES, ZS, 8, 2 * N), f32(ZS - 1, *chunk), f32(*chunk), f32(*chunk),
            f32(16, N), f32(3, 7, 16, N), f32(3, 16, N), f32(*tile), f32(*chunk), dma((9,)),
            pltpu.VMEM((SLOTS, N, N), BF16), pltpu.VMEM((2 * N, 2 * N), BF16), pltpu.VMEM((2 * N, 2 * N), BF16), f32(N, 2 * N),
            dma((8,)), dma((3,)), dma, dma, dma,
            dma((4,)), dma((4,)), dma((4, 2)), dma((4,)), dma((4,)), dma((4,)),
            dma((7,)), dma((7,)), dma, dma,
            dma((4,)), dma((4,)), dma((4,)), dma((4, 2)), dma((4,)), dma((4,)),
            dma, dma, dma((7,)), dma((7,)), dma, dma, dma((3, 7)), dma((3, 7)),
        ],
        compiler_params=pltpu.CompilerParams(collective_id=0, has_side_effects=True),
        name="ptycho",
    )(potential, probe, amplitudes, row_offset, col_offset, counts, forward, inverse, kern)
    return pl.pallas_call(
        finish,
        out_shape=tuple(jax.ShapeDtypeStruct(shape, F32) for shape in (tile, (1, *chunk))),
        in_specs=[hbm, hbm, hbm],
        out_specs=(hbm, hbm),
        scratch_shapes=[f32(*tile), f32(1, *chunk), f32(8, N), dma((SLICES + 2,)), dma((SLICES + 1,))],
        name="scale",
    )(obj, pgrad, scale)


def solution(mesh):
    placed = (
        P(None, None, "group", "pos"),
        P("group", None, "pos", None),
        P("group", "pos", None, None, None),
        P("group", "pos", None),
        P("group", "pos", None),
        P("group", "pos"),
    )
    return jax.shard_map(
        body,
        mesh=mesh,
        in_specs=placed,
        out_specs=(P(None, None, "group", "pos"), P("group", None, "pos", None)),
        check_vma=False,
    )
```

```python
import math

import jax
import jax.numpy as jnp
import numpy as np
from jax import lax
from jax.experimental import pallas as pl
from jax.experimental.pallas import tpu as pltpu
from jax.sharding import PartitionSpec as P

PROP = 0.25
REG = 0.1
N = 128
MODES = 4
SLICES = 4
SLOTS = 3
ROWS = 192
XS, YL, ZS = 4, 4, 8
F32 = jnp.float32
BF16 = jnp.bfloat16


def tables():
    idx = np.arange(N, dtype=np.int32)
    prod = (idx[:, None] * idx[None, :] % N).astype(np.float32)
    angle = np.float32(2.0 * math.pi / N) * prod
    root = np.float32(math.sqrt(N))
    cosv = np.cos(angle.astype(np.float64)).astype(np.float32) / root
    sinv = np.sin(angle.astype(np.float64)).astype(np.float32) / root
    forward = np.concatenate([np.concatenate([cosv, -sinv], 1), np.concatenate([sinv, cosv], 1)], 0)
    inverse = np.concatenate([np.concatenate([cosv, sinv], 1), np.concatenate([-sinv, cosv], 1)], 0)
    return jnp.asarray(forward).astype(BF16), jnp.asarray(inverse).astype(BF16)


def propagator():
    idx = np.arange(N, dtype=np.int32)
    freq = np.where(idx < N // 2, idx, idx - N).astype(np.float32)
    factor = np.float32(-2.0 * math.pi * PROP / N)
    phase = factor * (freq[:, None] * freq[:, None] + freq[None, :] * freq[None, :])
    phase = phase.astype(np.float32).astype(np.float64)
    return jnp.asarray(np.concatenate([np.cos(phase), np.sin(phase)], 1).astype(np.float32))


def cmul(a, b):
    return a[0] * b[0] - a[1] * b[1], a[0] * b[1] + a[1] * b[0]


def cmulc(a, b):
    return a[0] * b[0] + a[1] * b[1], a[0] * b[1] - a[1] * b[0]


def dft(waves, right, left):
    rows = [jnp.concatenate([re.astype(BF16), im.astype(BF16)], 1) for re, im in waves]
    first = jnp.dot(jnp.concatenate(rows, 0), right, preferred_element_type=F32).astype(BF16)
    cols = []
    for m in range(len(waves)):
        part = first[m * N : (m + 1) * N]
        cols.append(jnp.concatenate([part[:, :N], part[:, N:]], 0))
    second = jnp.dot(left, jnp.concatenate(cols, 1), preferred_element_type=F32)
    return [(second[:N, m * N : (m + 1) * N], second[N:, m * N : (m + 1) * N]) for m in range(len(waves))]


def kernel(
    pot, probe, amps_in, row_in, col_in, cnt_in, fwd_hbm, inv_hbm, kern_hbm,
    out_obj, out_probe, out_scale,
    n0, n1, n2, n3, c0, c1, c2, c3, gn, gc, rbuf, xbuf, sbuf, amps, amps_out, metav, meta_out, meta,
    pbuf, psi, wav, tr, gp, pgr, px, pzr, pown, pfin,
    mis, misr, smis, stage, chunk, stage_sem, amps_raw, fwd_in, inv_in, kern_in,
    loc_sem, s_misc, r_probe, r_meta, r_amp,
    s_n, r_n, s_c, r_c, s_f, r_f, s_pz, r_pz, s_pf, r_pf,
    s_x, r_x, s_r, r_r, s_rn, r_rn, s_px, r_px, s_pq, r_pq, s_po, r_po, s_m, r_m,
):
    nbuf = (n0, n1, n2, n3)
    cbuf = (c0, c1, c2, c3)
    g = lax.axis_index("group")
    pos = lax.axis_index("pos")
    x, yl, c = g // 8, (g // 2) % 4, g % 2
    z, h = pos // 2, pos % 2
    oh = 1 - h
    oc = 1 - c
    nat = c == h
    guest = c != h
    keep = jnp.where(nat, 0, 1)
    give = 1 - keep
    dz = jnp.where(h == 0, ZS - 1, 1)

    def dev(xx, yy, hh, zz, cc):
        return {"group": xx * 8 + yy * 2 + cc, "pos": zz * 2 + hh}

    def remote(src, dst, send, recv, to):
        return pltpu.make_async_remote_copy(src_ref=src, dst_ref=dst, send_sem=send, recv_sem=recv, device_id=to)

    def at_z(k):
        return lax.rem(z + k, ZS)

    sibling = dev(x, yl, h, z, oc)
    ring_z = [dev(x, yl, h, at_z(k), c) for k in range(1, ZS)]
    ring_y = []
    for k in range(1, 8):
        y = lax.rem(h * 4 + yl + k, 8)
        ring_y.append(dev(x, y % 4, y // 4, z, c))
    ring_x = []
    for k in range(1, 8):
        q = lax.rem(x * 2 + c + k, 8)
        ring_x.append(dev(q // 2, yl, h, z, q % 2))
    partners = ring_z + ring_y + ring_x
    partners += [dev(x, yl, oh, z, oc), dev(x, yl, h, at_z(1), oc), dev(x, yl, h, at_z(ZS - 1), oc)]

    barrier = pltpu.get_barrier_semaphore()
    for partner in partners:
        pl.semaphore_signal(barrier, inc=1, device_id=partner)

    own_pot = [pltpu.make_async_copy(pot.at[s], stage.at[s], stage_sem.at[s]) for s in range(SLICES)]
    own_p = pltpu.make_async_copy(probe.at[0], chunk, stage_sem.at[4])
    own_p.start()
    for s in range(SLICES):
        own_pot[s].start()

    lane = lax.broadcasted_iota(jnp.int32, (8, N), 1)
    packed = jnp.zeros((8, N), jnp.int32)
    for p in range(SLOTS):
        packed = jnp.where(lane == p, row_in[0, 0, p], packed)
        packed = jnp.where(lane == SLOTS + p, col_in[0, 0, p], packed)
    packed = jnp.where(lane == 2 * SLOTS, cnt_in[0, 0], packed)
    meta_out[...] = packed
    own_a = pltpu.make_async_copy(amps_in.at[0, 0], amps_raw, stage_sem.at[5])
    consts = [pltpu.make_async_copy(src, dst, stage_sem.at[6 + i]) for i, (src, dst) in enumerate(((fwd_hbm, fwd_in), (inv_hbm, inv_in), (kern_hbm, kern_in)))]
    own_a.start()
    for q in consts:
        q.start()

    pl.semaphore_wait(barrier, len(partners))

    def half_of(ref, hh):
        return ref.at[:, :, pl.ds(pl.multiple_of(hh * 8, 8), 8), :]

    def chunk_of(ref, zz, hh):
        return ref.at[:, zz, pl.ds(pl.multiple_of(hh * 8, 8), 8), :]

    to_probe = remote(chunk, chunk_of(pbuf, z, h), s_misc.at[0], r_probe, dev(x, yl, oh, z, oc))
    to_meta = remote(meta_out, metav, s_misc.at[1], r_meta, dev(x, yl, oh, z, 1))
    to_amp = remote(amps_out, amps, s_misc.at[2], r_amp, dev(x, yl, oh, z, 1))
    to_metan = remote(meta_out, metav, s_misc.at[1], r_meta, dev(x, yl, h, at_z(1), 0))
    to_ampn = remote(amps_out, amps, s_misc.at[2], r_amp, dev(x, yl, h, at_z(1), 0))
    to_n = [remote(stage.at[s], nbuf[s], s_n.at[s], r_n.at[s], dev(x, yl, h, lax.rem(z + dz, ZS), oc)) for s in range(SLICES)]
    to_c = [
        [remote(stage.at[s, ch], cbuf[s].at[ch], s_c.at[s, ch], r_c.at[s], dev(x, yl, oh, z, c if ch == 0 else oc)) for ch in range(2)]
        for s in range(SLICES)
    ]
    own_probe = [remote(chunk, chunk_of(pbuf, z, c), s_pz.at[k], r_pz.at[k], ring_z[k]) for k in range(ZS - 1)]
    got_probe = [remote(chunk_of(pbuf, z, c), chunk_of(pbuf, z, c), s_pz.at[k], r_pz.at[k], ring_z[k]) for k in range(ZS - 1)]
    loc_n = [pltpu.make_async_copy(stage.at[s], nbuf[s], loc_sem.at[s]) for s in range(SLICES)]
    loc_p = pltpu.make_async_copy(chunk, chunk_of(pbuf, z, c), loc_sem.at[4])
    loc_a = pltpu.make_async_copy(amps_out, amps, loc_sem.at[5])
    loc_m = pltpu.make_async_copy(meta_out, metav, loc_sem.at[6])
    loc_s = pltpu.make_async_copy(metav, meta, loc_sem.at[7])
    here = jnp.logical_and(nat, h == 0)
    along = jnp.logical_and(nat, h == 1)

    @pl.when(guest)
    def _():
        to_meta.start()

    @pl.when(along)
    def _():
        to_metan.start()

    @pl.when(here)
    def _():
        loc_m.start()

    own_p.wait()

    @pl.when(guest)
    def _():
        to_probe.start()

    own_pot[0].wait()

    @pl.when(guest)
    def _():
        for ch in range(2):
            to_c[0][ch].start()

    @pl.when(nat)
    def _():
        to_n[0].start()
        for k in (0, 6, 1, 5, 2, 4, 3):
            own_probe[k].start()
        loc_p.start()
        loc_n[0].start()

    for s in range(1, SLICES):
        own_pot[s].wait()

        @pl.when(guest)
        def _(s=s):
            for ch in range(2):
                to_c[s][ch].start()

        @pl.when(nat)
        def _(s=s):
            loc_n[s].start()

    own_a.wait()
    for p in range(SLOTS):
        amps_out[p] = amps_raw[p].astype(F32)

    @pl.when(guest)
    def _():
        to_amp.start()

    @pl.when(here)
    def _():
        loc_a.start()

    gp[...] = jnp.zeros_like(gp)
    for q in consts:
        q.wait()

    @pl.when(here)
    def _():
        loc_m.wait()

    @pl.when(jnp.logical_not(here))
    def _():
        to_meta.wait_recv()

    loc_s.start()

    @pl.when(guest)
    def _():
        to_probe.wait_recv()
        for k in (0, 6, 1, 5, 2, 4, 3):
            got_probe[k].start()

    @pl.when(nat)
    def _():
        loc_p.wait()

    loc_s.wait()

    fwd_c = [remote(cbuf[s].at[keep], cbuf[s].at[keep], s_f.at[s], r_f.at[s], sibling) for s in range(SLICES)]
    got_c = [remote(cbuf[s].at[keep], cbuf[s].at[keep], s_f.at[s], r_c.at[s], sibling) for s in range(SLICES)]

    def pass_on(s):
        got_c[s].wait_recv()
        fwd_c[s].start()

    last = jnp.logical_or(
        jnp.logical_and(jnp.logical_and(h == 0, c == 1), z == ZS - 1),
        jnp.logical_and(jnp.logical_and(h == 1, c == 0), z == 0),
    )
    alive = jnp.where(last, 0, 1)

    def masks(p, rows):
        col = meta[0, SLOTS + p]
        spot = lax.broadcasted_iota(jnp.int32, (rows, N), 1)
        n_lo = jnp.where(c == 0, col, 0)
        n_hi = jnp.where(c == 0, N, col * alive)
        c_lo = jnp.where(c == 0, 0, col)
        c_hi = jnp.where(c == 0, col * alive, N)
        in_n = jnp.logical_and(spot >= n_lo, spot < n_hi)
        in_c = jnp.logical_and(spot >= c_lo, spot < c_hi)
        return in_n, in_c, col

    def transmit(s):
        @pl.when(nat)
        def _():
            loc_n[s].wait()

        @pl.when(guest)
        def _():
            to_n[s].wait_recv()

        fwd_c[s].wait_recv()

        def one(p, carry):
            in_n, in_c, col = masks(p, N)
            row = meta[0, p]
            shift = lax.rem(N - col, N)
            parts = []
            for ch in range(2):
                near = nbuf[s][ch, pl.ds(row, N), :]
                far = cbuf[s][ch, pl.ds(row, N), :]
                both = jnp.where(in_n, near, jnp.where(in_c, far, 0.0))
                parts.append(pltpu.roll(both, shift, 1))
            mag = jnp.exp(-parts[1])
            tr[s, p, 0] = mag * jnp.cos(parts[0])
            tr[s, p, 1] = mag * jnp.sin(parts[0])
            return carry

        lax.fori_loop(0, SLOTS, one, 0, unroll=True)

    def pair(ref, *at):
        return ref[(*at, slice(None), slice(0, N))], ref[(*at, slice(None), slice(N, 2 * N))]

    def put(ref, value, *at):
        ref[(*at, slice(None), slice(0, N))] = value[0]
        ref[(*at, slice(None), slice(N, 2 * N))] = value[1]

    def psi_at(s, p, m):
        if s:
            return pair(psi, s - 1, p, m)
        whole = pbuf[m].reshape(N, 2 * N)
        return whole[:, 0:N], whole[:, N : 2 * N]

    def trans_at(s, p):
        return tr[s, p, 0], tr[s, p, 1]

    def prop(s):
        def one(p, carry):
            t = trans_at(s, p)
            kern = pair(kern_in)
            waves = dft([cmul(t, psi_at(s, p, m)) for m in range(MODES)], fwd_in[...], inv_in[...])
            waves = dft([cmul(kern, w) for w in waves], inv_in[...], fwd_in[...])
            for m in range(MODES):
                put(psi, waves[m], s, p, m)
            return carry

        lax.fori_loop(0, SLOTS, one, 0, unroll=True)

    pass_on(0)

    @pl.when(nat)
    def _():
        to_n[1].start()

    transmit(0)
    for k in range(ZS - 1):
        own_probe[k].wait_recv()
    fwd_p = remote(half_of(pbuf, c), half_of(pbuf, c), s_pf, r_pf, sibling)
    fwd_p.start()
    pass_on(1)
    fwd_p.wait_recv()

    @pl.when(nat)
    def _():
        for s in range(2, SLICES):
            to_n[s].start()

    @pl.when(along)
    def _():
        to_ampn.start()

    prop(0)
    pass_on(2)
    transmit(1)
    prop(1)
    pass_on(3)
    transmit(2)
    prop(2)
    transmit(3)

    count = meta[0, 2 * SLOTS]
    mis[0:8, :] = jnp.zeros((8, N), F32)
    mis[8:16, :] = jnp.zeros((8, N), F32) + count.astype(F32)

    def spectrum(p, carry):
        t = trans_at(SLICES - 1, p)
        far = dft([cmul(t, psi_at(SLICES - 1, p, m)) for m in range(MODES)], fwd_in[...], inv_in[...])
        for m in range(MODES):
            put(wav, far[m], p, m)
        return carry

    lax.fori_loop(0, SLOTS, spectrum, 0, unroll=True)

    @pl.when(here)
    def _():
        loc_a.wait()

    @pl.when(jnp.logical_not(here))
    def _():
        to_amp.wait_recv()

    def detect(p, carry):
        weight = jnp.where(p < count, 1.0, 0.0)
        far = [pair(wav, p, m) for m in range(MODES)]
        inten = far[0][0] * far[0][0] + far[0][1] * far[0][1]
        for m in range(1, MODES):
            inten = inten + (far[m][0] * far[m][0] + far[m][1] * far[m][1])
        model = jnp.sqrt(inten + REG)
        seen = amps[p]
        diff = model - seen
        sq = weight * (diff * diff)
        part = sq[0:8]
        for r in range(1, N // 8):
            part = part + sq[r * 8 : r * 8 + 8]
        mis[0:8, :] = mis[0:8, :] + part
        ratio = weight * (1.0 - seen / model)
        waves = dft([(w[0] * ratio, w[1] * ratio) for w in far], inv_in[...], fwd_in[...])
        for m in range(MODES):
            put(wav, waves[m], p, m)
        return carry

    lax.fori_loop(0, SLOTS, detect, 0, unroll=True)

    def spread(step, ring):
        return [remote(smis.at[step], misr.at[step, k], s_m.at[step, k], r_m.at[step, k], ring[k]) for k in range(7)]

    spreads = [spread(i, ring) for i, ring in enumerate((ring_z, ring_x, ring_y))]

    def send_mis(step):
        smis[step] = mis[...]
        for q in spreads[step]:
            q.start()

    def take_mis(step):
        total = mis[...]
        for k, q in enumerate(spreads[step]):
            q.wait_recv()
            total = total + misr[step, k]
        mis[...] = total

    send_mis(0)

    give_x = [remote(gc.at[s, give], xbuf.at[s], s_x.at[s], r_x.at[s], sibling) for s in range(SLICES)]
    send_r = [remote(sbuf.at[s], rbuf.at[s, keep], s_r.at[s], r_r.at[s, keep], dev(x, yl, oh, z, h)) for s in range(SLICES)]
    got_r = [[remote(sbuf.at[s], rbuf.at[s, ch], s_r.at[s], r_r.at[s, ch], sibling) for ch in range(2)] for s in range(SLICES)]
    send_rn = [remote(gn.at[s], rbuf.at[s], s_rn.at[s], r_rn.at[s], dev(x, yl, h, lax.rem(z + ZS - dz, ZS), h)) for s in range(SLICES)]

    def patch_grad(s):
        gn[s] = jnp.zeros((2, ROWS, N), F32)
        gc[s] = jnp.zeros((2, ROWS, N), F32)

        def one(p, carry):
            t = trans_at(s, p)
            parts = [cmulc(psi_at(s, p, m), pair(wav, p, m)) for m in range(MODES)]
            tg = (parts[0][0] + parts[1][0] + parts[2][0] + parts[3][0], parts[0][1] + parts[1][1] + parts[2][1] + parts[3][1])
            q = cmulc(t, tg)
            in_n, in_c, col = masks(p, ROWS)
            row = meta[0, p]
            for ch, value in enumerate((q[1], -q[0])):
                gp[ch, 64 : 64 + N, :] = pltpu.roll(value, col, 1)
                placed = gp[ch, pl.ds(64 - row, ROWS), :]
                gn[s, ch] = gn[s, ch] + jnp.where(in_n, placed, 0.0)
                gc[s, ch] = gc[s, ch] + jnp.where(in_c, placed, 0.0)
            return carry

        lax.fori_loop(0, SLOTS, one, 0, unroll=True)
        give_x[s].start()

        @pl.when(jnp.logical_and(guest, s > 0))
        def _():
            send_rn[s].start()

    def back(s):
        def one(p, carry):
            t = trans_at(s, p)
            kern = pair(kern_in)
            waves = dft([cmulc(t, pair(wav, p, m)) for m in range(MODES)], fwd_in[...], inv_in[...])
            waves = dft([cmulc(kern, w) for w in waves], inv_in[...], fwd_in[...])
            for m in range(MODES):
                put(wav, waves[m], p, m)
            return carry

        lax.fori_loop(0, SLOTS, one, 0, unroll=True)

    def hand_over(s):
        give_x[s].wait_recv()
        sbuf[s] = gc[s, keep] + xbuf[s]
        send_r[s].start()

    for s in reversed(range(1, SLICES)):
        patch_grad(s)
        back(s)
        hand_over(s)
        if s == 2:
            take_mis(0)
            send_mis(1)

    pgr[...] = jnp.zeros_like(pgr)

    def probe_slot(p, carry):
        t = trans_at(0, p)
        for m in range(MODES):
            w = jnp.concatenate(cmulc(t, pair(wav, p, m)), 1)
            pgr[m] = pgr[m] + w.reshape(ZS, 16, 2 * N)
        return carry

    lax.fori_loop(0, SLOTS, probe_slot, 0)
    give_p = remote(half_of(pgr, oc), px, s_px, r_px, sibling)
    give_p.start()
    patch_grad(0)
    give_p.wait_recv()
    px[...] = px[...] + pgr[:, :, pl.ds(pl.multiple_of(c * 8, 8), 8), :]
    send_q = [remote(px.at[:, at_z(k)], pzr.at[k - 1], s_pq.at[k - 1], r_pq.at[k - 1], ring_z[k - 1]) for k in range(1, ZS)]
    for k in (3, 2, 4, 1, 5, 0, 6):
        send_q[k].start()

    @pl.when(guest)
    def _():
        send_rn[0].start()

    hand_over(0)
    take_mis(1)
    send_mis(2)
    for q in send_q:
        q.wait_recv()
    done = px[:, z]
    for k in range(ZS - 1):
        done = done + pzr[k]
    send_po = remote(pfin, pown, s_po, r_po, dev(x, yl, oh, z, h))

    @pl.when(guest)
    def _():
        pfin[...] = done
        send_po.start()

    out_n = [pltpu.make_async_copy(gn.at[s], out_obj.at[s], loc_sem.at[s]) for s in range(SLICES)]
    out_r = [pltpu.make_async_copy(rbuf.at[s], out_obj.at[s], loc_sem.at[s]) for s in range(SLICES)]

    @pl.when(nat)
    def _():
        out_probe[0] = done
        for s in reversed(range(SLICES)):
            send_rn[s].wait_recv()
            gn[s] = gn[s] + rbuf[s]
            out_n[s].start()

    @pl.when(guest)
    def _():
        for s in reversed(range(SLICES)):
            for ch in range(2):
                got_r[s][ch].wait_recv()
            out_r[s].start()
        send_po.wait_recv()
        out_probe[0] = pown[...]

    take_mis(2)
    total = mis[...]
    misfit = jnp.sum(jnp.sum(total[0:8], axis=0, keepdims=True), axis=1, keepdims=True)
    slots = total[8:9, 0:1]
    out_scale[...] = jnp.broadcast_to(1.0 / jnp.sqrt(misfit / (slots * N * N) + 1e-06), (8, N))

    @pl.when(guest)
    def _():
        to_probe.wait_send()
        to_meta.wait_send()
        to_amp.wait_send()
        for s in range(SLICES):
            for ch in range(2):
                to_c[s][ch].wait_send()
            send_rn[s].wait_send()
        send_po.wait_send()

    @pl.when(nat)
    def _():
        for s in range(SLICES):
            to_n[s].wait_send()

    @pl.when(along)
    def _():
        to_metan.wait_send()
        to_ampn.wait_send()

    for k in range(ZS - 1):
        own_probe[k].wait_send()
        send_q[k].wait_send()
        for step in range(3):
            spreads[step][k].wait_send()
    fwd_p.wait_send()
    give_p.wait_send()
    for s in range(SLICES):
        out_n[s].wait()
        fwd_c[s].wait_send()
        give_x[s].wait_send()
        send_r[s].wait_send()


def finish(obj, pgrad, scale, out_obj, out_probe, held, held_probe, factor, in_sem, out_sem):
    loads = [pltpu.make_async_copy(scale, factor, in_sem.at[SLICES])]
    loads += [pltpu.make_async_copy(obj.at[s], held.at[s], in_sem.at[s]) for s in range(SLICES)]
    loads.append(pltpu.make_async_copy(pgrad, held_probe, in_sem.at[SLICES + 1]))
    stores = [pltpu.make_async_copy(held.at[s], out_obj.at[s], out_sem.at[s]) for s in range(SLICES)]
    stores.append(pltpu.make_async_copy(held_probe, out_probe, out_sem.at[SLICES]))
    for load in loads:
        load.start()
    loads[0].wait()
    by = factor[0:1, 0:1]
    for s in range(SLICES):
        loads[s + 1].wait()
        held[s] = held[s] * by
        stores[s].start()
    loads[-1].wait()
    held_probe[...] = held_probe[...] * by
    stores[-1].start()
    for store in stores:
        store.wait()


def body(potential, probe, amplitudes, row_offset, col_offset, counts):
    forward, inverse = tables()
    kern = propagator()
    vmem = pl.BlockSpec(memory_space=pltpu.VMEM)
    smem = pl.BlockSpec(memory_space=pltpu.SMEM)
    hbm = pl.BlockSpec(memory_space=pltpu.HBM)
    dma = pltpu.SemaphoreType.DMA
    tile = (SLICES, 2, ROWS, N)
    wave = (MODES, N, 2 * N)
    chunk = (MODES, 8, 2 * N)

    def f32(*shape):
        return pltpu.VMEM(shape, F32)

    obj, pgrad, scale = pl.pallas_call(
        kernel,
        out_shape=tuple(jax.ShapeDtypeStruct(shape, F32) for shape in (tile, (1, *chunk), (8, N))),
        in_specs=[hbm, hbm, hbm, smem, smem, smem, hbm, hbm, hbm],
        out_specs=(hbm, vmem, vmem),
        scratch_shapes=[
            *[f32(*tile[1:])] * 8, f32(*tile), f32(*tile), f32(*tile),
            f32(SLICES, ROWS, N), f32(SLICES, ROWS, N),
            f32(SLOTS, N, N), f32(SLOTS, N, N),
            pltpu.VMEM((8, N), jnp.int32), pltpu.VMEM((8, N), jnp.int32), pltpu.SMEM((8, N), jnp.int32),
            f32(MODES, ZS, 16, 2 * N), f32(SLICES - 1, SLOTS, *wave), f32(SLOTS, *wave),
            f32(SLICES, SLOTS, 2, N, N), f32(2, 256, N),
            f32(MODES, ZS, 16, 2 * N), f32(MODES, ZS, 8, 2 * N), f32(ZS - 1, *chunk), f32(*chunk), f32(*chunk),
            f32(16, N), f32(3, 7, 16, N), f32(3, 16, N), f32(*tile), f32(*chunk), dma((9,)),
            pltpu.VMEM((SLOTS, N, N), BF16), pltpu.VMEM((2 * N, 2 * N), BF16), pltpu.VMEM((2 * N, 2 * N), BF16), f32(N, 2 * N),
            dma((8,)), dma((3,)), dma, dma, dma,
            dma((4,)), dma((4,)), dma((4, 2)), dma((4,)), dma((4,)), dma((4,)),
            dma((7,)), dma((7,)), dma, dma,
            dma((4,)), dma((4,)), dma((4,)), dma((4, 2)), dma((4,)), dma((4,)),
            dma, dma, dma((7,)), dma((7,)), dma, dma, dma((3, 7)), dma((3, 7)),
        ],
        compiler_params=pltpu.CompilerParams(collective_id=0, has_side_effects=True),
        name="ptycho",
    )(potential, probe, amplitudes, row_offset, col_offset, counts, forward, inverse, kern)
    return pl.pallas_call(
        finish,
        out_shape=tuple(jax.ShapeDtypeStruct(shape, F32) for shape in (tile, (1, *chunk))),
        in_specs=[hbm, hbm, hbm],
        out_specs=(hbm, hbm),
        scratch_shapes=[f32(*tile), f32(1, *chunk), f32(8, N), dma((SLICES + 2,)), dma((SLICES + 1,))],
        name="scale",
    )(obj, pgrad, scale)


def solution(mesh):
    placed = (
        P(None, None, "group", "pos"),
        P("group", None, "pos", None),
        P("group", "pos", None, None, None),
        P("group", "pos", None),
        P("group", "pos", None),
        P("group", "pos"),
    )
    return jax.shard_map(
        body,
        mesh=mesh,
        in_specs=placed,
        out_specs=(P(None, None, "group", "pos"), P("group", None, "pos", None)),
        check_vma=False,
    )
```

```python
import math

import jax
import jax.numpy as jnp
import numpy as np
from jax import lax
from jax.experimental import pallas as pl
from jax.experimental.pallas import tpu as pltpu
from jax.sharding import PartitionSpec as P

PROP = 0.25
REG = 0.1
N = 128
MODES = 4
SLICES = 4
SLOTS = 3
ROWS = 192
XS, YL, ZS = 4, 4, 8
F32 = jnp.float32
BF16 = jnp.bfloat16


def tables():
    idx = np.arange(N, dtype=np.int32)
    prod = (idx[:, None] * idx[None, :] % N).astype(np.float32)
    angle = np.float32(2.0 * math.pi / N) * prod
    root = np.float32(math.sqrt(N))
    cosv = np.cos(angle.astype(np.float64)).astype(np.float32) / root
    sinv = np.sin(angle.astype(np.float64)).astype(np.float32) / root
    forward = np.concatenate([np.concatenate([cosv, -sinv], 1), np.concatenate([sinv, cosv], 1)], 0)
    inverse = np.concatenate([np.concatenate([cosv, sinv], 1), np.concatenate([-sinv, cosv], 1)], 0)
    return jnp.asarray(forward).astype(BF16), jnp.asarray(inverse).astype(BF16)


def propagator():
    idx = np.arange(N, dtype=np.int32)
    freq = np.where(idx < N // 2, idx, idx - N).astype(np.float32)
    factor = np.float32(-2.0 * math.pi * PROP / N)
    phase = factor * (freq[:, None] * freq[:, None] + freq[None, :] * freq[None, :])
    phase = phase.astype(np.float32).astype(np.float64)
    return jnp.asarray(np.concatenate([np.cos(phase), np.sin(phase)], 1).astype(np.float32))


def cmul(a, b):
    return a[0] * b[0] - a[1] * b[1], a[0] * b[1] + a[1] * b[0]


def cmulc(a, b):
    return a[0] * b[0] + a[1] * b[1], a[0] * b[1] - a[1] * b[0]


def dft(waves, right, left):
    rows = [jnp.concatenate([re.astype(BF16), im.astype(BF16)], 1) for re, im in waves]
    first = jnp.dot(jnp.concatenate(rows, 0), right, preferred_element_type=F32).astype(BF16)
    cols = []
    for m in range(len(waves)):
        part = first[m * N : (m + 1) * N]
        cols.append(jnp.concatenate([part[:, :N], part[:, N:]], 0))
    second = jnp.dot(left, jnp.concatenate(cols, 1), preferred_element_type=F32)
    return [(second[:N, m * N : (m + 1) * N], second[N:, m * N : (m + 1) * N]) for m in range(len(waves))]


def kernel(
    pot, probe, amps_in, row_hbm, col_hbm, cnt_hbm, fwd_hbm, inv_hbm, kern_hbm,
    out_obj, out_probe, out_scale,
    n0, n1, n2, n3, c0, c1, c2, c3, gn, gc, rbuf, xbuf, sbuf, amps, amps_out, metav, meta_out, meta,
    pbuf, psi, wav, tr, gp, pgr, px, pzr, pown, pfin,
    mis, misr, smis, stage, chunk, stage_sem, amps_raw, fwd_in, inv_in, kern_in, row_in, col_in, cnt_in,
    loc_sem, s_misc, r_probe, r_meta, r_amp,
    s_n, r_n, s_c, r_c, s_f, r_f, s_pz, r_pz, s_pf, r_pf,
    s_x, r_x, s_r, r_r, s_rn, r_rn, s_px, r_px, s_pq, r_pq, s_po, r_po, s_m, r_m,
):
    nbuf = (n0, n1, n2, n3)
    cbuf = (c0, c1, c2, c3)
    g = lax.axis_index("group")
    pos = lax.axis_index("pos")
    x, yl, c = g // 8, (g // 2) % 4, g % 2
    z, h = pos // 2, pos % 2
    oh = 1 - h
    oc = 1 - c
    nat = c == h
    guest = c != h
    keep = jnp.where(nat, 0, 1)
    give = 1 - keep
    dz = jnp.where(h == 0, ZS - 1, 1)

    def dev(xx, yy, hh, zz, cc):
        return {"group": xx * 8 + yy * 2 + cc, "pos": zz * 2 + hh}

    def remote(src, dst, send, recv, to):
        return pltpu.make_async_remote_copy(src_ref=src, dst_ref=dst, send_sem=send, recv_sem=recv, device_id=to)

    def at_z(k):
        return lax.rem(z + k, ZS)

    sibling = dev(x, yl, h, z, oc)
    ring_z = [dev(x, yl, h, at_z(k), c) for k in range(1, ZS)]
    ring_y = []
    for k in range(1, 8):
        y = lax.rem(h * 4 + yl + k, 8)
        ring_y.append(dev(x, y % 4, y // 4, z, c))
    ring_x = []
    for k in range(1, 8):
        q = lax.rem(x * 2 + c + k, 8)
        ring_x.append(dev(q // 2, yl, h, z, q % 2))
    partners = ring_z + ring_y + ring_x
    partners += [dev(x, yl, oh, z, oc), dev(x, yl, h, at_z(1), oc), dev(x, yl, h, at_z(ZS - 1), oc)]

    barrier = pltpu.get_barrier_semaphore()
    for partner in partners:
        pl.semaphore_signal(barrier, inc=1, device_id=partner)

    own_pot = [pltpu.make_async_copy(pot.at[s], stage.at[s], stage_sem.at[s]) for s in range(SLICES)]
    own_p = pltpu.make_async_copy(probe.at[0], chunk, stage_sem.at[4])
    scalars = [pltpu.make_async_copy(src, dst, stage_sem.at[9 + i]) for i, (src, dst) in enumerate(((row_hbm, row_in), (col_hbm, col_in), (cnt_hbm, cnt_in)))]
    for q in scalars:
        q.start()
    own_p.start()
    for s in range(SLICES):
        own_pot[s].start()

    own_a = pltpu.make_async_copy(amps_in.at[0, 0], amps_raw, stage_sem.at[5])
    consts = [pltpu.make_async_copy(src, dst, stage_sem.at[6 + i]) for i, (src, dst) in enumerate(((fwd_hbm, fwd_in), (inv_hbm, inv_in), (kern_hbm, kern_in)))]
    own_a.start()
    for q in consts:
        q.start()

    lane = lax.broadcasted_iota(jnp.int32, (8, N), 1)
    packed = jnp.zeros((8, N), jnp.int32)
    for q in scalars:
        q.wait()
    for p in range(SLOTS):
        packed = jnp.where(lane == p, row_in[0, 0, p], packed)
        packed = jnp.where(lane == SLOTS + p, col_in[0, 0, p], packed)
    packed = jnp.where(lane == 2 * SLOTS, cnt_in[0, 0], packed)
    meta_out[...] = packed
    pl.semaphore_wait(barrier, len(partners))

    def half_of(ref, hh):
        return ref.at[:, :, pl.ds(pl.multiple_of(hh * 8, 8), 8), :]

    def chunk_of(ref, zz, hh):
        return ref.at[:, zz, pl.ds(pl.multiple_of(hh * 8, 8), 8), :]

    to_probe = remote(chunk, chunk_of(pbuf, z, h), s_misc.at[0], r_probe, dev(x, yl, oh, z, oc))
    to_meta = remote(meta_out, metav, s_misc.at[1], r_meta, dev(x, yl, oh, z, 1))
    to_amp = remote(amps_out, amps, s_misc.at[2], r_amp, dev(x, yl, oh, z, 1))
    to_metan = remote(meta_out, metav, s_misc.at[1], r_meta, dev(x, yl, h, at_z(1), 0))
    to_ampn = remote(amps_out, amps, s_misc.at[2], r_amp, dev(x, yl, h, at_z(1), 0))
    to_n = [remote(stage.at[s], nbuf[s], s_n.at[s], r_n.at[s], dev(x, yl, h, lax.rem(z + dz, ZS), oc)) for s in range(SLICES)]
    to_c = [
        [remote(stage.at[s, ch], cbuf[s].at[ch], s_c.at[s, ch], r_c.at[s], dev(x, yl, oh, z, c if ch == 0 else oc)) for ch in range(2)]
        for s in range(SLICES)
    ]
    own_probe = [remote(chunk, chunk_of(pbuf, z, c), s_pz.at[k], r_pz.at[k], ring_z[k]) for k in range(ZS - 1)]
    got_probe = [remote(chunk_of(pbuf, z, c), chunk_of(pbuf, z, c), s_pz.at[k], r_pz.at[k], ring_z[k]) for k in range(ZS - 1)]
    loc_n = [pltpu.make_async_copy(stage.at[s], nbuf[s], loc_sem.at[s]) for s in range(SLICES)]
    loc_p = pltpu.make_async_copy(chunk, chunk_of(pbuf, z, c), loc_sem.at[4])
    loc_a = pltpu.make_async_copy(amps_out, amps, loc_sem.at[5])
    loc_m = pltpu.make_async_copy(meta_out, metav, loc_sem.at[6])
    loc_s = pltpu.make_async_copy(metav, meta, loc_sem.at[7])
    here = jnp.logical_and(nat, h == 0)
    along = jnp.logical_and(nat, h == 1)

    @pl.when(guest)
    def _():
        to_meta.start()

    @pl.when(along)
    def _():
        to_metan.start()

    @pl.when(here)
    def _():
        loc_m.start()

    own_p.wait()

    @pl.when(guest)
    def _():
        to_probe.start()

    own_pot[0].wait()

    @pl.when(guest)
    def _():
        for ch in range(2):
            to_c[0][ch].start()

    @pl.when(nat)
    def _():
        to_n[0].start()
        for k in (0, 6, 1, 5, 2, 4, 3):
            own_probe[k].start()
        loc_p.start()
        loc_n[0].start()

    for s in range(1, SLICES):
        own_pot[s].wait()

        @pl.when(guest)
        def _(s=s):
            for ch in range(2):
                to_c[s][ch].start()

        @pl.when(nat)
        def _(s=s):
            loc_n[s].start()

    own_a.wait()
    for p in range(SLOTS):
        amps_out[p] = amps_raw[p].astype(F32)

    @pl.when(guest)
    def _():
        to_amp.start()

    @pl.when(here)
    def _():
        loc_a.start()

    gp[...] = jnp.zeros_like(gp)
    for q in consts:
        q.wait()

    @pl.when(here)
    def _():
        loc_m.wait()

    @pl.when(jnp.logical_not(here))
    def _():
        to_meta.wait_recv()

    loc_s.start()

    @pl.when(guest)
    def _():
        to_probe.wait_recv()
        for k in (0, 6, 1, 5, 2, 4, 3):
            got_probe[k].start()

    @pl.when(nat)
    def _():
        loc_p.wait()

    loc_s.wait()

    fwd_c = [remote(cbuf[s].at[keep], cbuf[s].at[keep], s_f.at[s], r_f.at[s], sibling) for s in range(SLICES)]
    got_c = [remote(cbuf[s].at[keep], cbuf[s].at[keep], s_f.at[s], r_c.at[s], sibling) for s in range(SLICES)]

    def pass_on(s):
        got_c[s].wait_recv()
        fwd_c[s].start()

    last = jnp.logical_or(
        jnp.logical_and(jnp.logical_and(h == 0, c == 1), z == ZS - 1),
        jnp.logical_and(jnp.logical_and(h == 1, c == 0), z == 0),
    )
    alive = jnp.where(last, 0, 1)

    def masks(p, rows):
        col = meta[0, SLOTS + p]
        spot = lax.broadcasted_iota(jnp.int32, (rows, N), 1)
        n_lo = jnp.where(c == 0, col, 0)
        n_hi = jnp.where(c == 0, N, col * alive)
        c_lo = jnp.where(c == 0, 0, col)
        c_hi = jnp.where(c == 0, col * alive, N)
        in_n = jnp.logical_and(spot >= n_lo, spot < n_hi)
        in_c = jnp.logical_and(spot >= c_lo, spot < c_hi)
        return in_n, in_c, col

    def transmit(s):
        @pl.when(nat)
        def _():
            loc_n[s].wait()

        @pl.when(guest)
        def _():
            to_n[s].wait_recv()

        fwd_c[s].wait_recv()

        def one(p, carry):
            in_n, in_c, col = masks(p, N)
            row = meta[0, p]
            shift = lax.rem(N - col, N)
            parts = []
            for ch in range(2):
                near = nbuf[s][ch, pl.ds(row, N), :]
                far = cbuf[s][ch, pl.ds(row, N), :]
                both = jnp.where(in_n, near, jnp.where(in_c, far, 0.0))
                parts.append(pltpu.roll(both, shift, 1))
            mag = jnp.exp(-parts[1])
            tr[s, p, 0] = mag * jnp.cos(parts[0])
            tr[s, p, 1] = mag * jnp.sin(parts[0])
            return carry

        lax.fori_loop(0, SLOTS, one, 0, unroll=True)

    def pair(ref, *at):
        return ref[(*at, slice(None), slice(0, N))], ref[(*at, slice(None), slice(N, 2 * N))]

    def put(ref, value, *at):
        ref[(*at, slice(None), slice(0, N))] = value[0]
        ref[(*at, slice(None), slice(N, 2 * N))] = value[1]

    def psi_at(s, p, m):
        if s:
            return pair(psi, s - 1, p, m)
        whole = pbuf[m].reshape(N, 2 * N)
        return whole[:, 0:N], whole[:, N : 2 * N]

    def trans_at(s, p):
        return tr[s, p, 0], tr[s, p, 1]

    def prop(s):
        def one(p, carry):
            t = trans_at(s, p)
            kern = pair(kern_in)
            waves = dft([cmul(t, psi_at(s, p, m)) for m in range(MODES)], fwd_in[...], inv_in[...])
            waves = dft([cmul(kern, w) for w in waves], inv_in[...], fwd_in[...])
            for m in range(MODES):
                put(psi, waves[m], s, p, m)
            return carry

        lax.fori_loop(0, SLOTS, one, 0, unroll=True)

    pass_on(0)

    @pl.when(nat)
    def _():
        to_n[1].start()

    transmit(0)
    for k in range(ZS - 1):
        own_probe[k].wait_recv()
    fwd_p = remote(half_of(pbuf, c), half_of(pbuf, c), s_pf, r_pf, sibling)
    fwd_p.start()
    pass_on(1)
    fwd_p.wait_recv()

    @pl.when(nat)
    def _():
        for s in range(2, SLICES):
            to_n[s].start()

    @pl.when(along)
    def _():
        to_ampn.start()

    prop(0)
    pass_on(2)
    transmit(1)
    prop(1)
    pass_on(3)
    transmit(2)
    prop(2)
    transmit(3)

    count = meta[0, 2 * SLOTS]
    mis[0:8, :] = jnp.zeros((8, N), F32)
    mis[8:16, :] = jnp.zeros((8, N), F32) + count.astype(F32)

    def spectrum(p, carry):
        t = trans_at(SLICES - 1, p)
        far = dft([cmul(t, psi_at(SLICES - 1, p, m)) for m in range(MODES)], fwd_in[...], inv_in[...])
        for m in range(MODES):
            put(wav, far[m], p, m)
        return carry

    lax.fori_loop(0, SLOTS, spectrum, 0, unroll=True)

    @pl.when(here)
    def _():
        loc_a.wait()

    @pl.when(jnp.logical_not(here))
    def _():
        to_amp.wait_recv()

    def detect(p, carry):
        weight = jnp.where(p < count, 1.0, 0.0)
        far = [pair(wav, p, m) for m in range(MODES)]
        inten = far[0][0] * far[0][0] + far[0][1] * far[0][1]
        for m in range(1, MODES):
            inten = inten + (far[m][0] * far[m][0] + far[m][1] * far[m][1])
        model = jnp.sqrt(inten + REG)
        seen = amps[p]
        diff = model - seen
        sq = weight * (diff * diff)
        part = sq[0:8]
        for r in range(1, N // 8):
            part = part + sq[r * 8 : r * 8 + 8]
        mis[0:8, :] = mis[0:8, :] + part
        ratio = weight * (1.0 - seen / model)
        waves = dft([(w[0] * ratio, w[1] * ratio) for w in far], inv_in[...], fwd_in[...])
        for m in range(MODES):
            put(wav, waves[m], p, m)
        return carry

    lax.fori_loop(0, SLOTS, detect, 0, unroll=True)

    def spread(step, ring):
        return [remote(smis.at[step], misr.at[step, k], s_m.at[step, k], r_m.at[step, k], ring[k]) for k in range(7)]

    spreads = [spread(i, ring) for i, ring in enumerate((ring_z, ring_x, ring_y))]

    def send_mis(step):
        smis[step] = mis[...]
        for q in spreads[step]:
            q.start()

    def take_mis(step):
        total = mis[...]
        for k, q in enumerate(spreads[step]):
            q.wait_recv()
            total = total + misr[step, k]
        mis[...] = total

    send_mis(0)

    give_x = [remote(gc.at[s, give], xbuf.at[s], s_x.at[s], r_x.at[s], sibling) for s in range(SLICES)]
    send_r = [remote(sbuf.at[s], rbuf.at[s, keep], s_r.at[s], r_r.at[s, keep], dev(x, yl, oh, z, h)) for s in range(SLICES)]
    got_r = [[remote(sbuf.at[s], rbuf.at[s, ch], s_r.at[s], r_r.at[s, ch], sibling) for ch in range(2)] for s in range(SLICES)]
    send_rn = [remote(gn.at[s], rbuf.at[s], s_rn.at[s], r_rn.at[s], dev(x, yl, h, lax.rem(z + ZS - dz, ZS), h)) for s in range(SLICES)]

    def patch_grad(s):
        gn[s] = jnp.zeros((2, ROWS, N), F32)
        gc[s] = jnp.zeros((2, ROWS, N), F32)

        def one(p, carry):
            t = trans_at(s, p)
            parts = [cmulc(psi_at(s, p, m), pair(wav, p, m)) for m in range(MODES)]
            tg = (parts[0][0] + parts[1][0] + parts[2][0] + parts[3][0], parts[0][1] + parts[1][1] + parts[2][1] + parts[3][1])
            q = cmulc(t, tg)
            in_n, in_c, col = masks(p, ROWS)
            row = meta[0, p]
            for ch, value in enumerate((q[1], -q[0])):
                gp[ch, 64 : 64 + N, :] = pltpu.roll(value, col, 1)
                placed = gp[ch, pl.ds(64 - row, ROWS), :]
                gn[s, ch] = gn[s, ch] + jnp.where(in_n, placed, 0.0)
                gc[s, ch] = gc[s, ch] + jnp.where(in_c, placed, 0.0)
            return carry

        lax.fori_loop(0, SLOTS, one, 0, unroll=True)
        give_x[s].start()

        @pl.when(jnp.logical_and(guest, s > 0))
        def _():
            send_rn[s].start()

    def back(s, first, last):
        def one(p, carry):
            t = trans_at(s, p)
            kern = pair(kern_in)
            waves = dft([cmulc(t, pair(wav, p, m)) for m in range(MODES)], fwd_in[...], inv_in[...])
            waves = dft([cmulc(kern, w) for w in waves], inv_in[...], fwd_in[...])
            for m in range(MODES):
                put(wav, waves[m], p, m)
            return carry

        lax.fori_loop(first, last, one, 0, unroll=True)

    def hand_over(s):
        give_x[s].wait_recv()
        sbuf[s] = gc[s, keep] + xbuf[s]
        send_r[s].start()

    for s in reversed(range(1, SLICES)):
        patch_grad(s)
        if s == SLICES - 1:
            back(s, 0, 2)
            hand_over(s)
            back(s, 2, SLOTS)
        else:
            back(s, 0, SLOTS)
            hand_over(s)

    pgr[...] = jnp.zeros_like(pgr)

    def probe_slot(p, carry):
        t = trans_at(0, p)
        for m in range(MODES):
            w = jnp.concatenate(cmulc(t, pair(wav, p, m)), 1)
            pgr[m] = pgr[m] + w.reshape(ZS, 16, 2 * N)
        return carry

    lax.fori_loop(0, SLOTS, probe_slot, 0)
    give_p = remote(half_of(pgr, oc), px, s_px, r_px, sibling)
    give_p.start()
    take_mis(0)
    send_mis(1)
    patch_grad(0)
    give_p.wait_recv()
    px[...] = px[...] + pgr[:, :, pl.ds(pl.multiple_of(c * 8, 8), 8), :]
    send_q = [remote(px.at[:, at_z(k)], pzr.at[k - 1], s_pq.at[k - 1], r_pq.at[k - 1], ring_z[k - 1]) for k in range(1, ZS)]
    for k in (3, 2, 4, 1, 5, 0, 6):
        send_q[k].start()

    @pl.when(guest)
    def _():
        send_rn[0].start()

    hand_over(0)
    take_mis(1)
    send_mis(2)
    for q in send_q:
        q.wait_recv()
    done = px[:, z]
    for k in range(ZS - 1):
        done = done + pzr[k]
    send_po = remote(pfin, pown, s_po, r_po, dev(x, yl, oh, z, h))

    @pl.when(guest)
    def _():
        pfin[...] = done
        send_po.start()

    out_n = [pltpu.make_async_copy(gn.at[s], out_obj.at[s], loc_sem.at[s]) for s in range(SLICES)]
    out_r = [pltpu.make_async_copy(rbuf.at[s], out_obj.at[s], loc_sem.at[s]) for s in range(SLICES)]

    @pl.when(nat)
    def _():
        out_probe[0] = done
        for s in reversed(range(SLICES)):
            send_rn[s].wait_recv()
            gn[s] = gn[s] + rbuf[s]
            out_n[s].start()

    @pl.when(guest)
    def _():
        for s in reversed(range(SLICES)):
            for ch in range(2):
                got_r[s][ch].wait_recv()
            out_r[s].start()
        send_po.wait_recv()
        out_probe[0] = pown[...]

    take_mis(2)
    total = mis[...]
    misfit = jnp.sum(jnp.sum(total[0:8], axis=0, keepdims=True), axis=1, keepdims=True)
    slots = total[8:9, 0:1]
    out_scale[...] = jnp.broadcast_to(1.0 / jnp.sqrt(misfit / (slots * N * N) + 1e-06), (8, N))

    @pl.when(guest)
    def _():
        to_probe.wait_send()
        to_meta.wait_send()
        to_amp.wait_send()
        for s in range(SLICES):
            for ch in range(2):
                to_c[s][ch].wait_send()
            send_rn[s].wait_send()
        send_po.wait_send()

    @pl.when(nat)
    def _():
        for s in range(SLICES):
            to_n[s].wait_send()

    @pl.when(along)
    def _():
        to_metan.wait_send()
        to_ampn.wait_send()

    for k in range(ZS - 1):
        own_probe[k].wait_send()
        send_q[k].wait_send()
        for step in range(3):
            spreads[step][k].wait_send()
    fwd_p.wait_send()
    give_p.wait_send()
    for s in range(SLICES):
        out_n[s].wait()
        fwd_c[s].wait_send()
        give_x[s].wait_send()
        send_r[s].wait_send()


def finish(obj, pgrad, scale, out_obj, out_probe, held, held_probe, factor, in_sem, out_sem):
    loads = [pltpu.make_async_copy(scale, factor, in_sem.at[SLICES])]
    loads += [pltpu.make_async_copy(obj.at[s], held.at[s], in_sem.at[s]) for s in range(SLICES)]
    loads.append(pltpu.make_async_copy(pgrad, held_probe, in_sem.at[SLICES + 1]))
    stores = [pltpu.make_async_copy(held.at[s], out_obj.at[s], out_sem.at[s]) for s in range(SLICES)]
    stores.append(pltpu.make_async_copy(held_probe, out_probe, out_sem.at[SLICES]))
    for load in loads:
        load.start()
    loads[0].wait()
    by = factor[0:1, 0:1]
    for s in range(SLICES):
        loads[s + 1].wait()
        held[s] = held[s] * by
        stores[s].start()
    loads[-1].wait()
    held_probe[...] = held_probe[...] * by
    stores[-1].start()
    for store in stores:
        store.wait()


def body(potential, probe, amplitudes, row_offset, col_offset, counts):
    forward, inverse = tables()
    kern = propagator()
    vmem = pl.BlockSpec(memory_space=pltpu.VMEM)
    hbm = pl.BlockSpec(memory_space=pltpu.HBM)
    dma = pltpu.SemaphoreType.DMA
    tile = (SLICES, 2, ROWS, N)
    wave = (MODES, N, 2 * N)
    chunk = (MODES, 8, 2 * N)

    def f32(*shape):
        return pltpu.VMEM(shape, F32)

    obj, pgrad, scale = pl.pallas_call(
        kernel,
        out_shape=tuple(jax.ShapeDtypeStruct(shape, F32) for shape in (tile, (1, *chunk), (8, N))),
        in_specs=[hbm] * 9,
        out_specs=(hbm, vmem, vmem),
        scratch_shapes=[
            *[f32(*tile[1:])] * 8, f32(*tile), f32(*tile), f32(*tile),
            f32(SLICES, ROWS, N), f32(SLICES, ROWS, N),
            f32(SLOTS, N, N), f32(SLOTS, N, N),
            pltpu.VMEM((8, N), jnp.int32), pltpu.VMEM((8, N), jnp.int32), pltpu.SMEM((8, N), jnp.int32),
            f32(MODES, ZS, 16, 2 * N), f32(SLICES - 1, SLOTS, *wave), f32(SLOTS, *wave),
            f32(SLICES, SLOTS, 2, N, N), f32(2, 256, N),
            f32(MODES, ZS, 16, 2 * N), f32(MODES, ZS, 8, 2 * N), f32(ZS - 1, *chunk), f32(*chunk), f32(*chunk),
            f32(16, N), f32(3, 7, 16, N), f32(3, 16, N), f32(*tile), f32(*chunk), dma((12,)),
            pltpu.VMEM((SLOTS, N, N), BF16), pltpu.VMEM((2 * N, 2 * N), BF16), pltpu.VMEM((2 * N, 2 * N), BF16), f32(N, 2 * N),
            pltpu.SMEM((1, 1, SLOTS), jnp.int32), pltpu.SMEM((1, 1, SLOTS), jnp.int32), pltpu.SMEM((1, 1), jnp.int32),
            dma((8,)), dma((3,)), dma, dma, dma,
            dma((4,)), dma((4,)), dma((4, 2)), dma((4,)), dma((4,)), dma((4,)),
            dma((7,)), dma((7,)), dma, dma,
            dma((4,)), dma((4,)), dma((4,)), dma((4, 2)), dma((4,)), dma((4,)),
            dma, dma, dma((7,)), dma((7,)), dma, dma, dma((3, 7)), dma((3, 7)),
        ],
        compiler_params=pltpu.CompilerParams(collective_id=0, has_side_effects=True),
        name="ptycho",
    )(potential, probe, amplitudes, row_offset, col_offset, counts, forward, inverse, kern)
    return pl.pallas_call(
        finish,
        out_shape=tuple(jax.ShapeDtypeStruct(shape, F32) for shape in (tile, (1, *chunk))),
        in_specs=[hbm, hbm, hbm],
        out_specs=(hbm, hbm),
        scratch_shapes=[f32(*tile), f32(1, *chunk), f32(8, N), dma((SLICES + 2,)), dma((SLICES + 1,))],
        name="scale",
    )(obj, pgrad, scale)


def solution(mesh):
    placed = (
        P(None, None, "group", "pos"),
        P("group", None, "pos", None),
        P("group", "pos", None, None, None),
        P("group", "pos", None),
        P("group", "pos", None),
        P("group", "pos"),
    )
    return jax.shard_map(
        body,
        mesh=mesh,
        in_specs=placed,
        out_specs=(P(None, None, "group", "pos"), P("group", None, "pos", None)),
        check_vma=False,
    )
```

```python
import math

import jax
import jax.numpy as jnp
import numpy as np
from jax import lax
from jax.experimental import pallas as pl
from jax.experimental.pallas import tpu as pltpu
from jax.sharding import PartitionSpec as P

PROP = 0.25
REG = 0.1
N = 128
MODES = 4
SLICES = 4
SLOTS = 3
ROWS = 192
XS, YL, ZS = 4, 4, 8
F32 = jnp.float32
BF16 = jnp.bfloat16


def tables():
    idx = np.arange(N, dtype=np.int32)
    prod = (idx[:, None] * idx[None, :] % N).astype(np.float32)
    angle = np.float32(2.0 * math.pi / N) * prod
    root = np.float32(math.sqrt(N))
    cosv = np.cos(angle.astype(np.float64)).astype(np.float32) / root
    sinv = np.sin(angle.astype(np.float64)).astype(np.float32) / root
    forward = np.concatenate([np.concatenate([cosv, -sinv], 1), np.concatenate([sinv, cosv], 1)], 0)
    inverse = np.concatenate([np.concatenate([cosv, sinv], 1), np.concatenate([-sinv, cosv], 1)], 0)
    return jnp.asarray(forward).astype(BF16), jnp.asarray(inverse).astype(BF16)


def propagator():
    idx = np.arange(N, dtype=np.int32)
    freq = np.where(idx < N // 2, idx, idx - N).astype(np.float32)
    factor = np.float32(-2.0 * math.pi * PROP / N)
    phase = factor * (freq[:, None] * freq[:, None] + freq[None, :] * freq[None, :])
    phase = phase.astype(np.float32).astype(np.float64)
    return jnp.asarray(np.concatenate([np.cos(phase), np.sin(phase)], 1).astype(np.float32))


def cmul(a, b):
    return a[0] * b[0] - a[1] * b[1], a[0] * b[1] + a[1] * b[0]


def cmulc(a, b):
    return a[0] * b[0] + a[1] * b[1], a[0] * b[1] - a[1] * b[0]


def dft(waves, right, left):
    rows = [jnp.concatenate([re.astype(BF16), im.astype(BF16)], 1) for re, im in waves]
    first = jnp.dot(jnp.concatenate(rows, 0), right, preferred_element_type=F32).astype(BF16)
    cols = []
    for m in range(len(waves)):
        part = first[m * N : (m + 1) * N]
        cols.append(jnp.concatenate([part[:, :N], part[:, N:]], 0))
    second = jnp.dot(left, jnp.concatenate(cols, 1), preferred_element_type=F32)
    return [(second[:N, m * N : (m + 1) * N], second[N:, m * N : (m + 1) * N]) for m in range(len(waves))]


def kernel(
    pot, probe, amps_in, row_hbm, col_hbm, cnt_hbm, fwd_hbm, inv_hbm, kern_hbm,
    out_obj, out_probe, out_scale,
    n0, n1, n2, n3, c0, c1, c2, c3, gn, gc, rbuf, xbuf, sbuf, amps, amps_out, metav, meta_out, meta,
    pbuf, psi, wav0, wav1, tr, gp, pgr, px, pzr, pown, pfin,
    mis, misr, smis, stage, chunk, stage_sem, amps_raw, fwd_in, inv_in, kern_in, row_in, col_in, cnt_in,
    loc_sem, s_misc, r_probe, r_meta, r_amp,
    s_n, r_n, s_c, r_c, s_f, r_f, s_pz, r_pz, s_pf, r_pf,
    s_x, r_x, s_r, r_r, s_rn, r_rn, s_px, r_px, s_pq, r_pq, s_po, r_po, s_m, r_m,
):
    nbuf = (n0, n1, n2, n3)
    cbuf = (c0, c1, c2, c3)
    g = lax.axis_index("group")
    pos = lax.axis_index("pos")
    x, yl, c = g // 8, (g // 2) % 4, g % 2
    z, h = pos // 2, pos % 2
    oh = 1 - h
    oc = 1 - c
    nat = c == h
    guest = c != h
    keep = jnp.where(nat, 0, 1)
    give = 1 - keep
    dz = jnp.where(h == 0, ZS - 1, 1)

    def dev(xx, yy, hh, zz, cc):
        return {"group": xx * 8 + yy * 2 + cc, "pos": zz * 2 + hh}

    def remote(src, dst, send, recv, to):
        return pltpu.make_async_remote_copy(src_ref=src, dst_ref=dst, send_sem=send, recv_sem=recv, device_id=to)

    def at_z(k):
        return lax.rem(z + k, ZS)

    sibling = dev(x, yl, h, z, oc)
    ring_z = [dev(x, yl, h, at_z(k), c) for k in range(1, ZS)]
    ring_y = []
    for k in range(1, 8):
        y = lax.rem(h * 4 + yl + k, 8)
        ring_y.append(dev(x, y % 4, y // 4, z, c))
    ring_x = []
    for k in range(1, 8):
        q = lax.rem(x * 2 + c + k, 8)
        ring_x.append(dev(q // 2, yl, h, z, q % 2))
    partners = ring_z + ring_y + ring_x
    partners += [dev(x, yl, oh, z, oc), dev(x, yl, h, at_z(1), oc), dev(x, yl, h, at_z(ZS - 1), oc)]

    barrier = pltpu.get_barrier_semaphore()
    for partner in partners:
        pl.semaphore_signal(barrier, inc=1, device_id=partner)

    own_pot = [pltpu.make_async_copy(pot.at[s], stage.at[s], stage_sem.at[s]) for s in range(SLICES)]
    own_p = pltpu.make_async_copy(probe.at[0], chunk, stage_sem.at[4])
    scalars = [pltpu.make_async_copy(src, dst, stage_sem.at[9 + i]) for i, (src, dst) in enumerate(((row_hbm, row_in), (col_hbm, col_in), (cnt_hbm, cnt_in)))]
    for q in scalars:
        q.start()
    own_p.start()
    for s in range(SLICES):
        own_pot[s].start()

    own_a = pltpu.make_async_copy(amps_in.at[0, 0], amps_raw, stage_sem.at[5])
    consts = [pltpu.make_async_copy(src, dst, stage_sem.at[6 + i]) for i, (src, dst) in enumerate(((fwd_hbm, fwd_in), (inv_hbm, inv_in), (kern_hbm, kern_in)))]
    own_a.start()
    for q in consts:
        q.start()

    lane = lax.broadcasted_iota(jnp.int32, (8, N), 1)
    packed = jnp.zeros((8, N), jnp.int32)
    for q in scalars:
        q.wait()
    for p in range(SLOTS):
        packed = jnp.where(lane == p, row_in[0, 0, p], packed)
        packed = jnp.where(lane == SLOTS + p, col_in[0, 0, p], packed)
    packed = jnp.where(lane == 2 * SLOTS, cnt_in[0, 0], packed)
    meta_out[...] = packed
    pl.semaphore_wait(barrier, len(partners))

    def half_of(ref, hh):
        return ref.at[:, :, pl.ds(pl.multiple_of(hh * 8, 8), 8), :]

    def chunk_of(ref, zz, hh):
        return ref.at[:, zz, pl.ds(pl.multiple_of(hh * 8, 8), 8), :]

    to_probe = remote(chunk, chunk_of(pbuf, z, h), s_misc.at[0], r_probe, dev(x, yl, oh, z, oc))
    to_meta = remote(meta_out, metav, s_misc.at[1], r_meta, dev(x, yl, oh, z, 1))
    to_amp = remote(amps_out, amps, s_misc.at[2], r_amp, dev(x, yl, oh, z, 1))
    to_metan = remote(meta_out, metav, s_misc.at[1], r_meta, dev(x, yl, h, at_z(1), 0))
    to_ampn = remote(amps_out, amps, s_misc.at[2], r_amp, dev(x, yl, h, at_z(1), 0))
    to_n = [remote(stage.at[s], nbuf[s], s_n.at[s], r_n.at[s], dev(x, yl, h, lax.rem(z + dz, ZS), oc)) for s in range(SLICES)]
    to_c = [
        [remote(stage.at[s, ch], cbuf[s].at[ch], s_c.at[s, ch], r_c.at[s], dev(x, yl, oh, z, c if ch == 0 else oc)) for ch in range(2)]
        for s in range(SLICES)
    ]
    own_probe = [remote(chunk, chunk_of(pbuf, z, c), s_pz.at[k], r_pz.at[k], ring_z[k]) for k in range(ZS - 1)]
    got_probe = [remote(chunk_of(pbuf, z, c), chunk_of(pbuf, z, c), s_pz.at[k], r_pz.at[k], ring_z[k]) for k in range(ZS - 1)]
    loc_n = [pltpu.make_async_copy(stage.at[s], nbuf[s], loc_sem.at[s]) for s in range(SLICES)]
    loc_p = pltpu.make_async_copy(chunk, chunk_of(pbuf, z, c), loc_sem.at[4])
    loc_a = pltpu.make_async_copy(amps_out, amps, loc_sem.at[5])
    loc_m = pltpu.make_async_copy(meta_out, metav, loc_sem.at[6])
    loc_s = pltpu.make_async_copy(metav, meta, loc_sem.at[7])
    here = jnp.logical_and(nat, h == 0)
    along = jnp.logical_and(nat, h == 1)

    @pl.when(guest)
    def _():
        to_meta.start()

    @pl.when(along)
    def _():
        to_metan.start()

    @pl.when(here)
    def _():
        loc_m.start()

    own_p.wait()

    @pl.when(guest)
    def _():
        to_probe.start()

    own_pot[0].wait()

    @pl.when(guest)
    def _():
        for ch in range(2):
            to_c[0][ch].start()

    @pl.when(nat)
    def _():
        to_n[0].start()
        for k in (0, 6, 1, 5, 2, 4, 3):
            own_probe[k].start()
        loc_p.start()
        loc_n[0].start()

    for s in range(1, SLICES):
        own_pot[s].wait()

        @pl.when(guest)
        def _(s=s):
            for ch in range(2):
                to_c[s][ch].start()

        @pl.when(nat)
        def _(s=s):
            loc_n[s].start()

    own_a.wait()
    for p in range(SLOTS):
        amps_out[p] = amps_raw[p].astype(F32)

    @pl.when(guest)
    def _():
        to_amp.start()

    @pl.when(here)
    def _():
        loc_a.start()

    gp[...] = jnp.zeros_like(gp)
    for q in consts:
        q.wait()

    @pl.when(here)
    def _():
        loc_m.wait()

    @pl.when(jnp.logical_not(here))
    def _():
        to_meta.wait_recv()

    loc_s.start()

    @pl.when(guest)
    def _():
        to_probe.wait_recv()
        for k in (0, 6, 1, 5, 2, 4, 3):
            got_probe[k].start()

    @pl.when(nat)
    def _():
        loc_p.wait()

    loc_s.wait()

    fwd_c = [remote(cbuf[s].at[keep], cbuf[s].at[keep], s_f.at[s], r_f.at[s], sibling) for s in range(SLICES)]
    got_c = [remote(cbuf[s].at[keep], cbuf[s].at[keep], s_f.at[s], r_c.at[s], sibling) for s in range(SLICES)]

    def pass_on(s):
        got_c[s].wait_recv()
        fwd_c[s].start()

    last = jnp.logical_or(
        jnp.logical_and(jnp.logical_and(h == 0, c == 1), z == ZS - 1),
        jnp.logical_and(jnp.logical_and(h == 1, c == 0), z == 0),
    )
    alive = jnp.where(last, 0, 1)

    def masks(p, rows):
        col = meta[0, SLOTS + p]
        spot = lax.broadcasted_iota(jnp.int32, (rows, N), 1)
        n_lo = jnp.where(c == 0, col, 0)
        n_hi = jnp.where(c == 0, N, col * alive)
        c_lo = jnp.where(c == 0, 0, col)
        c_hi = jnp.where(c == 0, col * alive, N)
        in_n = jnp.logical_and(spot >= n_lo, spot < n_hi)
        in_c = jnp.logical_and(spot >= c_lo, spot < c_hi)
        return in_n, in_c, col

    def transmit(s):
        @pl.when(nat)
        def _():
            loc_n[s].wait()

        @pl.when(guest)
        def _():
            to_n[s].wait_recv()

        fwd_c[s].wait_recv()

        def one(p, carry):
            in_n, in_c, col = masks(p, N)
            row = meta[0, p]
            shift = lax.rem(N - col, N)
            parts = []
            for ch in range(2):
                near = nbuf[s][ch, pl.ds(row, N), :]
                far = cbuf[s][ch, pl.ds(row, N), :]
                both = jnp.where(in_n, near, jnp.where(in_c, far, 0.0))
                parts.append(pltpu.roll(both, shift, 1))
            mag = jnp.exp(-parts[1])
            tr[s, p, 0] = mag * jnp.cos(parts[0])
            tr[s, p, 1] = mag * jnp.sin(parts[0])
            return carry

        lax.fori_loop(0, SLOTS, one, 0, unroll=True)

    def pair(ref, *at):
        return ref[(*at, slice(None), slice(0, N))], ref[(*at, slice(None), slice(N, 2 * N))]

    def put(ref, value, *at):
        ref[(*at, slice(None), slice(0, N))] = value[0]
        ref[(*at, slice(None), slice(N, 2 * N))] = value[1]

    def psi_at(s, p, m):
        if s:
            return pair(psi, s - 1, p, m)
        whole = pbuf[m].reshape(N, 2 * N)
        return whole[:, 0:N], whole[:, N : 2 * N]

    def trans_at(s, p):
        return tr[s, p, 0], tr[s, p, 1]

    def prop(s):
        def one(p, carry):
            t = trans_at(s, p)
            kern = pair(kern_in)
            waves = dft([cmul(t, psi_at(s, p, m)) for m in range(MODES)], fwd_in[...], inv_in[...])
            waves = dft([cmul(kern, w) for w in waves], inv_in[...], fwd_in[...])
            for m in range(MODES):
                put(psi, waves[m], s, p, m)
            return carry

        lax.fori_loop(0, SLOTS, one, 0, unroll=True)

    pass_on(0)

    @pl.when(nat)
    def _():
        to_n[1].start()

    transmit(0)
    for k in range(ZS - 1):
        own_probe[k].wait_recv()
    fwd_p = remote(half_of(pbuf, c), half_of(pbuf, c), s_pf, r_pf, sibling)
    fwd_p.start()
    pass_on(1)
    fwd_p.wait_recv()

    @pl.when(nat)
    def _():
        for s in range(2, SLICES):
            to_n[s].start()

    @pl.when(along)
    def _():
        to_ampn.start()

    prop(0)
    pass_on(2)
    transmit(1)
    prop(1)
    pass_on(3)
    transmit(2)
    prop(2)
    transmit(3)

    count = meta[0, 2 * SLOTS]
    mis[0:8, :] = jnp.zeros((8, N), F32)
    mis[8:16, :] = jnp.zeros((8, N), F32) + count.astype(F32)

    wavs = (wav0, wav1)
    wav = wavs[(SLICES - 1) % 2]

    def spectrum(p, carry):
        t = trans_at(SLICES - 1, p)
        far = dft([cmul(t, psi_at(SLICES - 1, p, m)) for m in range(MODES)], fwd_in[...], inv_in[...])
        for m in range(MODES):
            put(wav, far[m], p, m)
        return carry

    lax.fori_loop(0, SLOTS, spectrum, 0, unroll=True)

    @pl.when(here)
    def _():
        loc_a.wait()

    @pl.when(jnp.logical_not(here))
    def _():
        to_amp.wait_recv()

    def detect(p, carry):
        weight = jnp.where(p < count, 1.0, 0.0)
        far = [pair(wav, p, m) for m in range(MODES)]
        inten = far[0][0] * far[0][0] + far[0][1] * far[0][1]
        for m in range(1, MODES):
            inten = inten + (far[m][0] * far[m][0] + far[m][1] * far[m][1])
        model = jnp.sqrt(inten + REG)
        seen = amps[p]
        diff = model - seen
        sq = weight * (diff * diff)
        part = sq[0:8]
        for r in range(1, N // 8):
            part = part + sq[r * 8 : r * 8 + 8]
        mis[0:8, :] = mis[0:8, :] + part
        ratio = weight * (1.0 - seen / model)
        waves = dft([(w[0] * ratio, w[1] * ratio) for w in far], inv_in[...], fwd_in[...])
        for m in range(MODES):
            put(wav, waves[m], p, m)
        return carry

    lax.fori_loop(0, SLOTS, detect, 0, unroll=True)

    def spread(step, ring):
        return [remote(smis.at[step], misr.at[step, k], s_m.at[step, k], r_m.at[step, k], ring[k]) for k in range(7)]

    spreads = [spread(i, ring) for i, ring in enumerate((ring_z, ring_x, ring_y))]

    def send_mis(step):
        smis[step] = mis[...]
        for q in spreads[step]:
            q.start()

    def take_mis(step):
        total = mis[...]
        for k, q in enumerate(spreads[step]):
            q.wait_recv()
            total = total + misr[step, k]
        mis[...] = total

    send_mis(0)

    give_x = [remote(gc.at[s, give], xbuf.at[s], s_x.at[s], r_x.at[s], sibling) for s in range(SLICES)]
    send_r = [remote(sbuf.at[s], rbuf.at[s, keep], s_r.at[s], r_r.at[s, keep], dev(x, yl, oh, z, h)) for s in range(SLICES)]
    got_r = [[remote(sbuf.at[s], rbuf.at[s, ch], s_r.at[s], r_r.at[s, ch], sibling) for ch in range(2)] for s in range(SLICES)]
    send_rn = [remote(gn.at[s], rbuf.at[s], s_rn.at[s], r_rn.at[s], dev(x, yl, h, lax.rem(z + ZS - dz, ZS), h)) for s in range(SLICES)]

    def patch_grad(s):
        gn[s] = jnp.zeros((2, ROWS, N), F32)
        gc[s] = jnp.zeros((2, ROWS, N), F32)

        def one(p, carry):
            t = trans_at(s, p)
            parts = [cmulc(psi_at(s, p, m), pair(wavs[s % 2], p, m)) for m in range(MODES)]
            tg = (parts[0][0] + parts[1][0] + parts[2][0] + parts[3][0], parts[0][1] + parts[1][1] + parts[2][1] + parts[3][1])
            q = cmulc(t, tg)
            in_n, in_c, col = masks(p, ROWS)
            row = meta[0, p]
            for ch, value in enumerate((q[1], -q[0])):
                gp[ch, 64 : 64 + N, :] = pltpu.roll(value, col, 1)
                placed = gp[ch, pl.ds(64 - row, ROWS), :]
                gn[s, ch] = gn[s, ch] + jnp.where(in_n, placed, 0.0)
                gc[s, ch] = gc[s, ch] + jnp.where(in_c, placed, 0.0)
            return carry

        lax.fori_loop(0, SLOTS, one, 0, unroll=True)
        give_x[s].start()

        @pl.when(jnp.logical_and(guest, s > 0))
        def _():
            send_rn[s].start()

    def back(s, first, last):
        def one(p, carry):
            t = trans_at(s, p)
            kern = pair(kern_in)
            waves = dft([cmulc(t, pair(wavs[s % 2], p, m)) for m in range(MODES)], fwd_in[...], inv_in[...])
            waves = dft([cmulc(kern, w) for w in waves], inv_in[...], fwd_in[...])
            for m in range(MODES):
                put(wavs[(s - 1) % 2], waves[m], p, m)
            return carry

        lax.fori_loop(first, last, one, 0, unroll=True)

    def hand_over(s):
        give_x[s].wait_recv()
        sbuf[s] = gc[s, keep] + xbuf[s]
        send_r[s].start()

    for s in reversed(range(1, SLICES)):
        if s > 1:
            patch_grad(s)
        if s == SLICES - 1:
            back(s, 0, 2)
            hand_over(s)
            back(s, 2, SLOTS)
        else:
            back(s, 0, SLOTS)
        if s == 2:
            hand_over(s)

    pgr[...] = jnp.zeros_like(pgr)

    def probe_slot(p, carry):
        t = trans_at(0, p)
        for m in range(MODES):
            w = jnp.concatenate(cmulc(t, pair(wavs[0], p, m)), 1)
            pgr[m] = pgr[m] + w.reshape(ZS, 16, 2 * N)
        return carry

    lax.fori_loop(0, SLOTS, probe_slot, 0)
    give_p = remote(half_of(pgr, oc), px, s_px, r_px, sibling)
    give_p.start()
    patch_grad(1)
    take_mis(0)
    send_mis(1)
    patch_grad(0)
    give_p.wait_recv()
    px[...] = px[...] + pgr[:, :, pl.ds(pl.multiple_of(c * 8, 8), 8), :]
    send_q = [remote(px.at[:, at_z(k)], pzr.at[k - 1], s_pq.at[k - 1], r_pq.at[k - 1], ring_z[k - 1]) for k in range(1, ZS)]
    for k in (3, 2, 4, 1, 5, 0, 6):
        send_q[k].start()

    @pl.when(guest)
    def _():
        send_rn[0].start()

    hand_over(1)
    hand_over(0)
    take_mis(1)
    send_mis(2)
    for q in send_q:
        q.wait_recv()
    done = px[:, z]
    for k in range(ZS - 1):
        done = done + pzr[k]
    send_po = remote(pfin, pown, s_po, r_po, dev(x, yl, oh, z, h))

    @pl.when(guest)
    def _():
        pfin[...] = done
        send_po.start()

    out_n = [pltpu.make_async_copy(gn.at[s], out_obj.at[s], loc_sem.at[s]) for s in range(SLICES)]
    out_r = [pltpu.make_async_copy(rbuf.at[s], out_obj.at[s], loc_sem.at[s]) for s in range(SLICES)]

    @pl.when(nat)
    def _():
        out_probe[0] = done
        for s in reversed(range(SLICES)):
            send_rn[s].wait_recv()
            gn[s] = gn[s] + rbuf[s]
            out_n[s].start()

    @pl.when(guest)
    def _():
        for s in reversed(range(SLICES)):
            for ch in range(2):
                got_r[s][ch].wait_recv()
            out_r[s].start()
        send_po.wait_recv()
        out_probe[0] = pown[...]

    take_mis(2)
    total = mis[...]
    misfit = jnp.sum(jnp.sum(total[0:8], axis=0, keepdims=True), axis=1, keepdims=True)
    slots = total[8:9, 0:1]
    out_scale[...] = jnp.broadcast_to(1.0 / jnp.sqrt(misfit / (slots * N * N) + 1e-06), (8, N))

    @pl.when(guest)
    def _():
        to_probe.wait_send()
        to_meta.wait_send()
        to_amp.wait_send()
        for s in range(SLICES):
            for ch in range(2):
                to_c[s][ch].wait_send()
            send_rn[s].wait_send()
        send_po.wait_send()

    @pl.when(nat)
    def _():
        for s in range(SLICES):
            to_n[s].wait_send()

    @pl.when(along)
    def _():
        to_metan.wait_send()
        to_ampn.wait_send()

    for k in range(ZS - 1):
        own_probe[k].wait_send()
        send_q[k].wait_send()
        for step in range(3):
            spreads[step][k].wait_send()
    fwd_p.wait_send()
    give_p.wait_send()
    for s in range(SLICES):
        out_n[s].wait()
        fwd_c[s].wait_send()
        give_x[s].wait_send()
        send_r[s].wait_send()


def finish(obj, pgrad, scale, out_obj, out_probe, held, held_probe, factor, in_sem, out_sem):
    loads = [pltpu.make_async_copy(scale, factor, in_sem.at[SLICES])]
    loads += [pltpu.make_async_copy(obj.at[s], held.at[s], in_sem.at[s]) for s in range(SLICES)]
    loads.append(pltpu.make_async_copy(pgrad, held_probe, in_sem.at[SLICES + 1]))
    stores = [pltpu.make_async_copy(held.at[s], out_obj.at[s], out_sem.at[s]) for s in range(SLICES)]
    stores.append(pltpu.make_async_copy(held_probe, out_probe, out_sem.at[SLICES]))
    for load in loads:
        load.start()
    loads[0].wait()
    by = factor[0:1, 0:1]
    for s in range(SLICES):
        loads[s + 1].wait()
        held[s] = held[s] * by
        stores[s].start()
    loads[-1].wait()
    held_probe[...] = held_probe[...] * by
    stores[-1].start()
    for store in stores:
        store.wait()


def body(potential, probe, amplitudes, row_offset, col_offset, counts):
    forward, inverse = tables()
    kern = propagator()
    vmem = pl.BlockSpec(memory_space=pltpu.VMEM)
    hbm = pl.BlockSpec(memory_space=pltpu.HBM)
    dma = pltpu.SemaphoreType.DMA
    tile = (SLICES, 2, ROWS, N)
    wave = (MODES, N, 2 * N)
    chunk = (MODES, 8, 2 * N)

    def f32(*shape):
        return pltpu.VMEM(shape, F32)

    obj, pgrad, scale = pl.pallas_call(
        kernel,
        out_shape=tuple(jax.ShapeDtypeStruct(shape, F32) for shape in (tile, (1, *chunk), (8, N))),
        in_specs=[hbm] * 9,
        out_specs=(hbm, vmem, vmem),
        scratch_shapes=[
            *[f32(*tile[1:])] * 8, f32(*tile), f32(*tile), f32(*tile),
            f32(SLICES, ROWS, N), f32(SLICES, ROWS, N),
            f32(SLOTS, N, N), f32(SLOTS, N, N),
            pltpu.VMEM((8, N), jnp.int32), pltpu.VMEM((8, N), jnp.int32), pltpu.SMEM((8, N), jnp.int32),
            f32(MODES, ZS, 16, 2 * N), f32(SLICES - 1, SLOTS, *wave), f32(SLOTS, *wave), f32(SLOTS, *wave),
            f32(SLICES, SLOTS, 2, N, N), f32(2, 256, N),
            f32(MODES, ZS, 16, 2 * N), f32(MODES, ZS, 8, 2 * N), f32(ZS - 1, *chunk), f32(*chunk), f32(*chunk),
            f32(16, N), f32(3, 7, 16, N), f32(3, 16, N), f32(*tile), f32(*chunk), dma((12,)),
            pltpu.VMEM((SLOTS, N, N), BF16), pltpu.VMEM((2 * N, 2 * N), BF16), pltpu.VMEM((2 * N, 2 * N), BF16), f32(N, 2 * N),
            pltpu.SMEM((1, 1, SLOTS), jnp.int32), pltpu.SMEM((1, 1, SLOTS), jnp.int32), pltpu.SMEM((1, 1), jnp.int32),
            dma((8,)), dma((3,)), dma, dma, dma,
            dma((4,)), dma((4,)), dma((4, 2)), dma((4,)), dma((4,)), dma((4,)),
            dma((7,)), dma((7,)), dma, dma,
            dma((4,)), dma((4,)), dma((4,)), dma((4, 2)), dma((4,)), dma((4,)),
            dma, dma, dma((7,)), dma((7,)), dma, dma, dma((3, 7)), dma((3, 7)),
        ],
        compiler_params=pltpu.CompilerParams(collective_id=0, has_side_effects=True),
        name="ptycho",
    )(potential, probe, amplitudes, row_offset, col_offset, counts, forward, inverse, kern)
    return pl.pallas_call(
        finish,
        out_shape=tuple(jax.ShapeDtypeStruct(shape, F32) for shape in (tile, (1, *chunk))),
        in_specs=[hbm, hbm, hbm],
        out_specs=(hbm, hbm),
        scratch_shapes=[f32(*tile), f32(1, *chunk), f32(8, N), dma((SLICES + 2,)), dma((SLICES + 1,))],
        name="scale",
    )(obj, pgrad, scale)


def solution(mesh):
    placed = (
        P(None, None, "group", "pos"),
        P("group", None, "pos", None),
        P("group", "pos", None, None, None),
        P("group", "pos", None),
        P("group", "pos", None),
        P("group", "pos"),
    )
    return jax.shard_map(
        body,
        mesh=mesh,
        in_specs=placed,
        out_specs=(P(None, None, "group", "pos"), P("group", None, "pos", None)),
        check_vma=False,
    )
```
